128 devices in a mesh: lat: 32 (over y, z, core), slot: 4 (over x).
Axes of the slice: x: 4, y: 4, z: 4, core: 2. Of those that a mesh axis runs over, the one named last changes fastest.
Arguments:
- seasonal_normals: bfloat16 [64, 8, 704, 1440], P('slot', None, 'lat'), may hold values from -24 to 24
- overlay_coarse_parallels: int32 [128, 10], P('lat'), may hold values from 0 to 703, as said below
- overlay_extent_factor: float32 [128, 10], P('lat'), may hold values from 0.2 to 1
- overlay_member_number: int32 [128], P('lat'), may hold values from 7 to 10
- verifying_seasonal_bin: int32 [128, 4], P('slot'), may hold values from 0 to 63
- prognosis_grid: bfloat16 [128, 4, 8, 128, 240], P('slot', None, None, 'lat'), may hold values from -6 to 6
- observed_analysis: bfloat16 [128, 4, 8, 128, 240], P('slot', None, None, 'lat'), may hold values from -6 to 6
Outputs:
- rmse_map: float32 [4, 8, 128, 240], P('slot', None, 'lat')
- acc_map: float32 [4, 8, 128, 240], P('slot', None, 'lat')
The draws below stay inside these ranges and needn't reach their ends.
Inputs may be any that keep to these rules, and one draw needn't show every extreme that they name: `overlay_coarse_parallels`: for k < overlay_member_number[t] the entries of row t are the consecutive source rows that target row t margins; later entries are padding and repeat live entries. With center(t) = ((2t + 1) * 704) // 256, every entry of row t lies in source rows max(center(t) - 5, 0) to min(center(t) + 4, 703).
All inputs are finite; a program needn't handle non-finite values.
Results may differ from the reference program's by a relative error of at most 0.00085.
Values may be sent and summed in bfloat16 or wider, within the bound.
No kernel may reach another device: no remote copies, remote signals or barrier semaphores. Data moves between devices by JAX's collectives and lax.ppermute only.
A program may use at most 256 MiB of HBM per device.

```python
import math
import jax
import jax.numpy as jnp
from jax import lax

SRC_LAT = 704
SRC_LON = 1440
DEST_PARALLELS = 128
DEST_MERIDIANS = 240
NUM_VARIABLES = 8
SEASONAL_BINS = 64
HORIZON_STEPS = 4
OVER = 10
INIT_DAYS = 128
TGT_TILE = 4


def margin_lists(key):
    target = jnp.arange(DEST_PARALLELS, dtype=jnp.int32)
    center = (2 * target + 1) * SRC_LAT // (2 * DEST_PARALLELS)
    below = jax.random.randint(jax.random.fold_in(key, 11), (DEST_PARALLELS,), 3, 6, dtype=jnp.int32)
    above = jax.random.randint(jax.random.fold_in(key, 12), (DEST_PARALLELS,), 3, 5, dtype=jnp.int32)
    below = jnp.where(target % TGT_TILE == 0, 5, below)
    above = jnp.where(target % TGT_TILE == TGT_TILE - 1, 4, above)
    first_row = jnp.maximum(center - below, 0)
    final_row = jnp.minimum(center + above, SRC_LAT - 1)
    final_row = jnp.minimum(jnp.maximum(final_row, first_row + 6), SRC_LAT - 1)
    first_row = jnp.maximum(jnp.minimum(first_row, final_row - 6), 0)
    length = final_row - first_row + 1
    entries = jnp.arange(OVER, dtype=jnp.int32)
    filler = jax.random.randint(jax.random.fold_in(key, 13), (DEST_PARALLELS, OVER), 0, 1 << 20, dtype=jnp.int32) % length[:, None]
    offset = jnp.where(entries[None, :] < length[:, None], entries[None, :], filler)
    source_rows = jnp.clip(first_row[:, None] + offset, 0, SRC_LAT - 1)
    return (source_rows.astype(jnp.int32), length.astype(jnp.int32))


def draw_overlay_coarse_parallels(key, part):
    return margin_lists(jax.random.fold_in(key, 7))[0]


def draw_overlay_member_number(key, part):
    return margin_lists(jax.random.fold_in(key, 7))[1]


def set_ends(result, rng, low, top_value):
    longest = result.shape.index(max(result.shape))
    spots = []
    for shift in (0, 1):
        where = [jax.random.randint(jax.random.fold_in(rng, axis), (), 0, length) for axis, length in enumerate(result.shape)]
        where[longest] = (where[longest] + shift) % result.shape[longest]
        spots.append(tuple(where))
    return result.at[spots[0]].set(low).at[spots[1]].set(top_value)


def steps_of(own_key, shape, pieces, least, top_value):
    factor_of, own = 1.0, jax.random.fold_in(own_key, 6)
    for axis_at, parts in pieces:
        draws = jnp.exp(jax.random.uniform(jax.random.fold_in(own, axis_at), (parts,), jnp.float32, least / len(pieces), top_value / len(pieces)))
        factor_of = factor_of * jnp.repeat(draws, shape[axis_at] // parts).reshape([-1 if axis == axis_at else 1 for axis in range(len(shape))])
    return factor_of


def normal_values(own_key, extent, spread, reach, pieces=(), held_as=jnp.bfloat16):
    array = jax.random.normal(own_key, extent, jnp.float32) * spread
    if len(pieces) > 0:
        array = steps_of(own_key, extent, pieces, -0.22, 0.18) * array
    return jnp.clip(array, min=-reach, max=reach).astype(held_as)


def setup_inputs(seed: int = 0) -> dict:
    key_of = jax.random.split(jax.random.key(seed), 8)
    seasonal_normals = normal_values(key_of[0], (SEASONAL_BINS, NUM_VARIABLES, SRC_LAT, SRC_LON), 4.0, 24.0, ((0, 4), (2, 32)))
    overlay_coarse_parallels = draw_overlay_coarse_parallels(jax.random.fold_in(key_of[7], 71), 0)
    overlay_extent_factor = jnp.clip(0.2 + 0.8 * jax.random.uniform(key_of[2], (DEST_PARALLELS, OVER), jnp.float32) ** steps_of(key_of[2], (DEST_PARALLELS, OVER), ((0, 32),), -0.2, 0.2), 0.2, 1.0)
    overlay_member_number = draw_overlay_member_number(jax.random.fold_in(key_of[7], 71), 0)
    verifying_seasonal_bin = set_ends(jax.random.randint(key_of[4], (INIT_DAYS, HORIZON_STEPS), 0, SEASONAL_BINS), jax.random.fold_in(key_of[4], 1), 0, SEASONAL_BINS - 1).astype(jnp.int32)
    prognosis_grid = normal_values(key_of[5], (INIT_DAYS, HORIZON_STEPS, NUM_VARIABLES, DEST_PARALLELS, DEST_MERIDIANS), 1.0, 6.0, ((0, 4), (3, 32)))
    observed_analysis = normal_values(key_of[6], (INIT_DAYS, HORIZON_STEPS, NUM_VARIABLES, DEST_PARALLELS, DEST_MERIDIANS), 1.0, 6.0, ((0, 4), (3, 32)))
    return dict(seasonal_normals=seasonal_normals, overlay_coarse_parallels=overlay_coarse_parallels, overlay_extent_factor=overlay_extent_factor, overlay_member_number=overlay_member_number, verifying_seasonal_bin=verifying_seasonal_bin, prognosis_grid=prognosis_grid, observed_analysis=observed_analysis)


def reference(seasonal_normals, overlay_coarse_parallels, overlay_extent_factor, overlay_member_number, verifying_seasonal_bin, prognosis_grid, observed_analysis):
    meridian_refinement = SRC_LON // DEST_MERIDIANS
    lon_mean = (lax.optimization_barrier(jnp.sum(seasonal_normals.reshape(SEASONAL_BINS, NUM_VARIABLES, SRC_LAT, DEST_MERIDIANS, meridian_refinement), axis=-1, dtype=jnp.float32)) * (1.0 / meridian_refinement)).astype(jnp.bfloat16)
    live_slots = jnp.arange(OVER, dtype=jnp.int32)[None, :] < overlay_member_number[:, None]
    raw_weight = jnp.where(live_slots, overlay_extent_factor, jnp.zeros_like(overlay_extent_factor))
    weight = raw_weight / lax.optimization_barrier(jnp.sum(raw_weight, axis=1, keepdims=True))
    climate = jnp.zeros((SEASONAL_BINS, NUM_VARIABLES, DEST_PARALLELS, DEST_MERIDIANS), jnp.float32)
    for entry in range(OVER):
        picked = jnp.take(lon_mean, overlay_coarse_parallels[:, entry].astype(jnp.int32), axis=2).astype(jnp.float32)
        climate = climate + weight[:, entry][None, None, :, None] * picked
    latitude = (jnp.arange(DEST_PARALLELS, dtype=jnp.float32) + 0.5) * (math.pi / DEST_PARALLELS) - 0.5 * math.pi
    cosine = jnp.cos(latitude)
    parallel_cosine_factor = cosine / jnp.mean(cosine)
    misfit_spread_record = []
    acc_list = []
    for horizon_position in range(HORIZON_STEPS):
        clim_valid = jnp.take(climate, verifying_seasonal_bin[:, horizon_position].astype(jnp.int32), axis=0)
        prognosis_snapshot = prognosis_grid[:, horizon_position].astype(jnp.float32)
        observed = observed_analysis[:, horizon_position].astype(jnp.float32)
        error = prognosis_snapshot - observed
        fore_anom = prognosis_snapshot - clim_valid
        true_anom = observed - clim_valid
        squared_misfit = lax.optimization_barrier(jnp.sum(error * error, axis=0))
        cross_sum = lax.optimization_barrier(jnp.sum(fore_anom * true_anom, axis=0))
        fore_sq = lax.optimization_barrier(jnp.sum(fore_anom * fore_anom, axis=0))
        true_sq = lax.optimization_barrier(jnp.sum(true_anom * true_anom, axis=0))
        misfit_spread_record.append(jnp.sqrt(parallel_cosine_factor[None, :, None] * squared_misfit / INIT_DAYS))
        acc_list.append(cross_sum / jnp.sqrt(fore_sq * true_sq + 1e-06))
    return (jnp.stack(misfit_spread_record, axis=0), jnp.stack(acc_list, axis=0))
```

```python
import math

import jax
import jax.numpy as jnp
import numpy as np
from jax import lax
from jax.experimental import pallas as pl
from jax.experimental.pallas import tpu as pltpu
from jax.sharding import PartitionSpec as P

SRC_LON = 1440
DEST_PARALLELS = 128
DEST_MERIDIANS = 240
FINE = SRC_LON // DEST_MERIDIANS
VARS = 8
BAND = 22
TILE = 4
OVER = 10
UP = 3
DOWN = 2
MID = BAND - UP - DOWN
ROWS = BAND + UP + DOWN
BINS = 16
DAYS = 32
SLOTS = 4
FLAT = VARS * TILE
CODE_RATE = 10.0
CODE_BASE = 120.0


def shifted(value, step):
    slots = lax.axis_size("slot")
    return lax.ppermute(value, "slot", [(i, (i + step) % slots) for i in range(slots)])


def lon_table():
    fine = np.arange(SRC_LON)[:, None] // FINE
    return jnp.asarray(fine == np.arange(DEST_MERIDIANS)[None, :], dtype=jnp.bfloat16)


def lon_mean(rows, table):
    flat = rows.reshape(-1, SRC_LON)
    total = jnp.dot(flat, table, preferred_element_type=jnp.float32)
    return (total * (1.0 / FINE)).astype(jnp.bfloat16).reshape(*rows.shape[:-1], DEST_MERIDIANS)


def edge_kernel(low_ref, high_ref, table_ref, down_ref, up_ref):
    table = table_ref[...]
    up_ref[...] = lon_mean(high_ref[...], table)
    down_ref[...] = lon_mean(low_ref[...], table)


def band_rows(chunk, first, count):
    sizes = (chunk, count, VARS, SRC_LON)
    return pl.BlockSpec(tuple(pl.Element(n) for n in sizes), lambda i: (i * chunk, first, 0, 0))


def edges(field, table):
    chunk = 4
    spec = lambda count: pl.BlockSpec(
        (chunk, count, VARS, DEST_MERIDIANS), lambda i: (i, 0, 0, 0)
    )
    shape = lambda count: jax.ShapeDtypeStruct((BINS, count, VARS, DEST_MERIDIANS), jnp.bfloat16)
    return pl.pallas_call(
        edge_kernel,
        grid=(BINS // chunk,),
        in_specs=[
            band_rows(chunk, 0, DOWN),
            band_rows(chunk, BAND - UP, UP),
            pl.BlockSpec((SRC_LON, DEST_MERIDIANS), lambda i: (0, 0)),
        ],
        out_specs=[spec(DOWN), spec(UP)],
        out_shape=[shape(DOWN), shape(UP)],
        name="edge_lon",
    )(field, field, table)


def mid_kernel(rows_ref, table_ref, out_ref):
    out_ref[...] = lon_mean(rows_ref[...], table_ref[...])


def middle(field, table):
    chunk = 2
    return pl.pallas_call(
        mid_kernel,
        grid=(BINS // chunk,),
        in_specs=[
            band_rows(chunk, DOWN, MID),
            pl.BlockSpec((SRC_LON, DEST_MERIDIANS), lambda i: (0, 0)),
        ],
        out_specs=pl.BlockSpec((chunk, MID, VARS, DEST_MERIDIANS), lambda i: (i, 0, 0, 0)),
        out_shape=jax.ShapeDtypeStruct((BINS, MID, VARS, DEST_MERIDIANS), jnp.bfloat16),
        name="mid_lon",
        cost_estimate=pl.CostEstimate(flops=2 * 10**9, bytes_accessed=8 * 10**6, transcendentals=0),
    )(field, table)


def encode(value):
    size = jnp.exp2(CODE_RATE * jnp.abs(value) - CODE_BASE)
    return jnp.where(value < 0, -size, size).astype(jnp.bfloat16)


def decode(code):
    wide = code.astype(jnp.float32)
    size = (jnp.log2(jnp.abs(wide)) + CODE_BASE) * (1.0 / CODE_RATE)
    return jnp.where(wide < 0, -size, size)


def weight_matrix(index_ref, extent_ref, count_ref):
    base = lax.axis_index("lat") * BAND - UP
    line = lax.broadcasted_iota(jnp.int32, (FLAT, ROWS * VARS), 0)
    lane = lax.broadcasted_iota(jnp.int32, (FLAT, ROWS * VARS), 1)
    place = jnp.where(line // TILE == lane % VARS, lane // VARS, -1)
    dense = jnp.zeros((FLAT, ROWS * VARS), jnp.float32)
    sums = jnp.ones((FLAT, ROWS * VARS), jnp.float32)
    for t in range(TILE):
        here = line % TILE == t
        spot = jnp.where(here, place, -1)
        total = jnp.float32(0.0)
        for k in range(OVER):
            value = jnp.where(k < count_ref[t], extent_ref[t, k], jnp.float32(0.0))
            total = total + value
            dense = dense + jnp.where(spot == index_ref[t, k] - base, value, 0.0)
        sums = jnp.where(here, total, sums)
    dense = dense / sums
    high = dense.astype(jnp.bfloat16)
    rest = dense - high.astype(jnp.float32)
    middle_part = rest.astype(jnp.bfloat16)
    low = (rest - middle_part.astype(jnp.float32)).astype(jnp.bfloat16)
    return jnp.concatenate([high, middle_part, low], axis=0)


def climate_kernel(
    index_ref, extent_ref, count_ref, below_ref, down_ref, mid_ref, up_ref, above_ref, code_ref
):
    weights = weight_matrix(index_ref, extent_ref, count_ref)
    for s in range(BINS):
        rows = jnp.concatenate(
            [below_ref[s], down_ref[s], mid_ref[s], up_ref[s], above_ref[s]], axis=0
        ).reshape(ROWS * VARS, DEST_MERIDIANS)
        parts = jnp.dot(weights, rows, preferred_element_type=jnp.float32)
        value = parts[:FLAT] + parts[FLAT : 2 * FLAT] + parts[2 * FLAT :]
        code_ref[s] = encode(value)


def climate_code(index, extent, count, below, down, mid, up, above):
    smem = pl.BlockSpec(memory_space=pltpu.SMEM)
    vmem = pl.BlockSpec(memory_space=pltpu.VMEM)
    return pl.pallas_call(
        climate_kernel,
        in_specs=[smem] * 3 + [vmem] * 5,
        out_specs=vmem,
        out_shape=jax.ShapeDtypeStruct((BINS, FLAT, DEST_MERIDIANS), jnp.bfloat16),
        name="climate",
    )(index, extent, count, below, down, mid, up, above)


def sums_kernel(
    bins_ref, own_ref, right_ref, far_low_ref, far_high_ref, left_ref, fore_ref, obs_ref,
    out_ref, clim_ref,
):
    slot = lax.axis_index("slot")
    lead = lax.rem(pl.program_id(0) + 1 + slot, SLOTS)

    @pl.when(pl.program_id(0) == 0)
    def _():
        half = BINS // 2
        clim_ref[:BINS] = decode(own_ref[...])
        clim_ref[BINS : 2 * BINS] = decode(right_ref[...])
        clim_ref[2 * BINS : 2 * BINS + half] = decode(far_low_ref[...])
        clim_ref[2 * BINS + half : 3 * BINS] = decode(far_high_ref[...])
        clim_ref[3 * BINS :] = decode(left_ref[...])

    half = VARS // 2
    lines = half * TILE
    for h in range(2):

        def step(d, sums):
            squared, cross, fore_sq, true_sq = sums
            fore = fore_ref[d, 0, h * half : (h + 1) * half].astype(jnp.float32)
            fore = fore.reshape(lines, DEST_MERIDIANS)
            obs = obs_ref[d, 0, h * half : (h + 1) * half].astype(jnp.float32)
            obs = obs.reshape(lines, DEST_MERIDIANS)
            wanted = bins_ref[lead, d]
            spot = (wanted // BINS - slot) % SLOTS * BINS + wanted % BINS
            clim = clim_ref[spot, h * lines : (h + 1) * lines]
            error = fore - obs
            fore_anom = fore - clim
            true_anom = obs - clim
            return (
                squared + error * error,
                cross + fore_anom * true_anom,
                fore_sq + fore_anom * fore_anom,
                true_sq + true_anom * true_anom,
            )

        zero = jnp.zeros((lines, DEST_MERIDIANS), jnp.float32)
        sums = lax.fori_loop(0, DAYS, step, (zero,) * 4, unroll=4)
        for n, value in enumerate(sums):
            out_ref[0, n, h * lines : (h + 1) * lines] = value


def skill_sums(bins, own, right, far_low, far_high, left, fore, obs):
    vmem = pl.BlockSpec(memory_space=pltpu.VMEM)
    days = pl.BlockSpec(
        (DAYS, 1, VARS, TILE, DEST_MERIDIANS),
        lambda i: (0, lax.rem(i + 1 + lax.axis_index("slot"), SLOTS), 0, 0, 0),
    )
    return pl.pallas_call(
        sums_kernel,
        grid=(SLOTS,),
        in_specs=[pl.BlockSpec(memory_space=pltpu.SMEM)] + [vmem] * 5 + [days] * 2,
        out_specs=pl.BlockSpec((1, 4, FLAT, DEST_MERIDIANS), lambda i: (i, 0, 0, 0)),
        out_shape=jax.ShapeDtypeStruct((SLOTS, 4, FLAT, DEST_MERIDIANS), jnp.float32),
        scratch_shapes=[pltpu.VMEM((SLOTS * BINS, FLAT, DEST_MERIDIANS), jnp.float32)],
        name="skill_sums",
    )(bins, own, right, far_low, far_high, left, fore, obs)


def maps_kernel(scale_ref, one_ref, two_ref, three_ref, own_ref, rmse_ref, acc_ref):
    lat = lax.axis_index("lat")
    total = own_ref[...] + one_ref[...] + two_ref[...] + three_ref[...]
    line = lax.broadcasted_iota(jnp.int32, (FLAT, DEST_MERIDIANS), 0)
    scale = jnp.zeros((FLAT, DEST_MERIDIANS), jnp.float32)
    for t in range(TILE):
        scale = jnp.where(line % TILE == t, scale_ref[lat * TILE + t], scale)
    days = DAYS * SLOTS
    rmse = jnp.sqrt(scale * total[0] / days)
    acc = total[1] / jnp.sqrt(total[2] * total[3] + 1e-06)
    rmse_ref[0] = rmse.reshape(VARS, TILE, DEST_MERIDIANS)
    acc_ref[0] = acc.reshape(VARS, TILE, DEST_MERIDIANS)


def maps(one, two, three, own):
    phi = (np.arange(DEST_PARALLELS, dtype=np.float32) + np.float32(0.5)) * np.float32(
        math.pi / DEST_PARALLELS
    ) - np.float32(0.5 * math.pi)
    cosine = np.cos(phi).astype(np.float32)
    scale = jnp.asarray(cosine / cosine.mean(dtype=np.float32))
    vmem = pl.BlockSpec(memory_space=pltpu.VMEM)
    shape = jax.ShapeDtypeStruct((1, VARS, TILE, DEST_MERIDIANS), jnp.float32)
    return pl.pallas_call(
        maps_kernel,
        in_specs=[pl.BlockSpec(memory_space=pltpu.SMEM)] + [vmem] * 4,
        out_specs=[vmem] * 2,
        out_shape=[shape] * 2,
        name="maps",
    )(scale, one, two, three, own)


def body(normals, index, extent, count, bins, prognosis, analysis):
    field = jnp.transpose(normals, (0, 2, 1, 3))
    table = lon_table()
    down, up = edges(field, table)
    devices = lax.axis_size("lat")
    below = lax.ppermute(up, "lat", [(i, i + 1) for i in range(devices - 1)])
    above = lax.ppermute(down, "lat", [(i + 1, i) for i in range(devices - 1)])
    mid = middle(field, table)
    own = climate_code(index, extent, count, below, down, mid, up, above)
    left = shifted(own, 1)
    right = shifted(own, -1)
    half = BINS // 2
    far_low = shifted(left[:half], 1)
    far_high = shifted(right[half:], -1)
    sums = skill_sums(
        jnp.transpose(bins), own, right, far_low, far_high, left, prognosis, analysis
    )
    two = shifted(sums[1], 2)
    one = shifted(sums[0], 1)
    three = shifted(sums[2], 3)
    return tuple(maps(one, two, three, sums[3]))


def solution(mesh):
    placed = (
        P("slot", None, "lat", None),
        P("lat", None),
        P("lat", None),
        P("lat"),
        P("slot", None),
        P("slot", None, None, "lat", None),
        P("slot", None, None, "lat", None),
    )
    return jax.shard_map(
        body,
        mesh=mesh,
        in_specs=placed,
        out_specs=(P("slot", None, "lat", None), P("slot", None, "lat", None)),
        check_vma=False,
    )
```

```python
import functools
import math

import jax
import jax.numpy as jnp
import numpy as np
from jax import lax
from jax.experimental import pallas as pl
from jax.experimental.pallas import tpu as pltpu
from jax.sharding import PartitionSpec as P

SRC_LON = 1440
DEST_PARALLELS = 128
DEST_MERIDIANS = 240
FINE = SRC_LON // DEST_MERIDIANS
VARS = 8
BAND = 22
TILE = 4
OVER = 10
UP = 3
DOWN = 2
MID = BAND - UP - DOWN
ROWS = BAND + UP + DOWN
BINS = 16
DAYS = 32
SLOTS = 4
FLAT = VARS * TILE
CODE_RATE = 10.0
CODE_BASE = 120.0


def shifted(value, step):
    slots = lax.axis_size("slot")
    return lax.ppermute(value, "slot", [(i, (i + step) % slots) for i in range(slots)])


def lon_table():
    fine = np.arange(SRC_LON)[:, None] // FINE
    return jnp.asarray(fine == np.arange(DEST_MERIDIANS)[None, :], dtype=jnp.bfloat16)


def lon_mean(rows, table):
    flat = rows.reshape(-1, SRC_LON)
    total = jnp.dot(flat, table, preferred_element_type=jnp.float32)
    return (total * (1.0 / FINE)).astype(jnp.bfloat16).reshape(*rows.shape[:-1], DEST_MERIDIANS)


def params(mebibytes):
    return pltpu.CompilerParams(vmem_limit_bytes=mebibytes * 1024 * 1024)


def cost(microseconds):
    return pl.CostEstimate(
        flops=0, bytes_accessed=int(microseconds * 3 * 10**6), transcendentals=0
    )


def edge_kernel(field_ref, table_ref, down_ref, up_ref, low_buf, high_buf, table_buf, sems):
    parts = low_buf.shape[0]
    size = BINS // parts
    load = pltpu.make_async_copy(table_ref, table_buf, sems.at[2 * parts])
    load.start()
    copies = []
    for n in range(parts):
        some = pl.ds(n * size, size)
        low = pltpu.make_async_copy(field_ref.at[some, pl.ds(0, DOWN)], low_buf.at[n], sems.at[n])
        high = pltpu.make_async_copy(
            field_ref.at[some, pl.ds(BAND - UP, UP)], high_buf.at[n], sems.at[parts + n]
        )
        low.start()
        high.start()
        copies.append((low, high))
    load.wait()
    for n in range(parts):
        low, high = copies[n]
        low.wait()
        down_ref[n * size : (n + 1) * size] = lon_mean(low_buf[n], table_buf[...])
        high.wait()
        up_ref[n * size : (n + 1) * size] = lon_mean(high_buf[n], table_buf[...])


def edges(field, table):
    parts = 2
    vmem = pl.BlockSpec(memory_space=pltpu.VMEM)
    hbm = pl.BlockSpec(memory_space=pl.ANY)
    shape = lambda count: jax.ShapeDtypeStruct((BINS, count, VARS, DEST_MERIDIANS), jnp.bfloat16)
    return pl.pallas_call(
        edge_kernel,
        in_specs=[hbm, hbm],
        out_specs=[vmem, vmem],
        out_shape=[shape(DOWN), shape(UP)],
        scratch_shapes=[
            pltpu.VMEM((parts, BINS // parts, DOWN, VARS, SRC_LON), jnp.bfloat16),
            pltpu.VMEM((parts, BINS // parts, UP, VARS, SRC_LON), jnp.bfloat16),
            pltpu.VMEM((SRC_LON, DEST_MERIDIANS), jnp.bfloat16),
            pltpu.SemaphoreType.DMA((2 * parts + 1,)),
        ],
        compiler_params=params(57),
        cost_estimate=cost(2),
        name="edge_lon",
    )(field, table)


def mid_kernel(field_ref, table_ref, out_ref, buf, table_buf, sems):
    parts = buf.shape[0]
    size = BINS // parts
    load = pltpu.make_async_copy(table_ref, table_buf, sems.at[parts])
    load.start()
    copies = []
    for n in range(parts):
        copy = pltpu.make_async_copy(
            field_ref.at[pl.ds(n * size, size), pl.ds(DOWN, MID)], buf.at[n], sems.at[n]
        )
        copy.start()
        copies.append(copy)
    load.wait()
    for n in range(parts):
        copies[n].wait()
        out_ref[n * size : (n + 1) * size] = lon_mean(buf[n], table_buf[...])


def middle(field, table):
    parts = 4
    hbm = pl.BlockSpec(memory_space=pl.ANY)
    return pl.pallas_call(
        mid_kernel,
        in_specs=[hbm, hbm],
        out_specs=pl.BlockSpec(memory_space=pltpu.VMEM),
        out_shape=jax.ShapeDtypeStruct((BINS, MID, VARS, DEST_MERIDIANS), jnp.bfloat16),
        scratch_shapes=[
            pltpu.VMEM((parts, BINS // parts, MID, VARS, SRC_LON), jnp.bfloat16),
            pltpu.VMEM((SRC_LON, DEST_MERIDIANS), jnp.bfloat16),
            pltpu.SemaphoreType.DMA((parts + 1,)),
        ],
        compiler_params=params(54),
        cost_estimate=cost(4),
        name="mid_lon",
    )(field, table)


def encode(value):
    size = jnp.exp2(CODE_RATE * jnp.abs(value) - CODE_BASE)
    return jnp.where(value < 0, -size, size).astype(jnp.bfloat16)


def decode(code):
    wide = code.astype(jnp.float32)
    size = (jnp.log2(jnp.abs(wide)) + CODE_BASE) * (1.0 / CODE_RATE)
    return jnp.where(wide < 0, -size, size)


def weight_matrix(index_ref, extent_ref, count_ref):
    base = lax.axis_index("lat") * BAND - UP
    line = lax.broadcasted_iota(jnp.int32, (FLAT, ROWS * VARS), 0)
    lane = lax.broadcasted_iota(jnp.int32, (FLAT, ROWS * VARS), 1)
    place = jnp.where(line // TILE == lane % VARS, lane // VARS, -1)
    dense = jnp.zeros((FLAT, ROWS * VARS), jnp.float32)
    sums = jnp.ones((FLAT, ROWS * VARS), jnp.float32)
    for t in range(TILE):
        here = line % TILE == t
        spot = jnp.where(here, place, -1)
        total = jnp.float32(0.0)
        for k in range(OVER):
            value = jnp.where(k < count_ref[t], extent_ref[t, k], jnp.float32(0.0))
            total = total + value
            dense = dense + jnp.where(spot == index_ref[t, k] - base, value, 0.0)
        sums = jnp.where(here, total, sums)
    dense = dense / sums
    high = dense.astype(jnp.bfloat16)
    rest = dense - high.astype(jnp.float32)
    middle_part = rest.astype(jnp.bfloat16)
    low = (rest - middle_part.astype(jnp.float32)).astype(jnp.bfloat16)
    return jnp.concatenate([high, middle_part, low], axis=0)


def climate_kernel(
    index_ref, extent_ref, count_ref, below_ref, down_ref, mid_ref, up_ref, above_ref, code_ref
):
    weights = weight_matrix(index_ref, extent_ref, count_ref)
    for s in range(BINS):
        rows = jnp.concatenate(
            [below_ref[s], down_ref[s], mid_ref[s], up_ref[s], above_ref[s]], axis=0
        ).reshape(ROWS * VARS, DEST_MERIDIANS)
        parts = jnp.dot(weights, rows, preferred_element_type=jnp.float32)
        value = parts[:FLAT] + parts[FLAT : 2 * FLAT] + parts[2 * FLAT :]
        code_ref[s] = encode(value)


def climate_code(index, extent, count, below, down, mid, up, above):
    smem = pl.BlockSpec(memory_space=pltpu.SMEM)
    vmem = pl.BlockSpec(memory_space=pltpu.VMEM)
    return pl.pallas_call(
        climate_kernel,
        in_specs=[smem] * 3 + [vmem] * 5,
        out_specs=vmem,
        out_shape=jax.ShapeDtypeStruct((BINS, FLAT, DEST_MERIDIANS), jnp.bfloat16),
        compiler_params=params(8),
        cost_estimate=cost(2),
        name="climate",
    )(index, extent, count, below, down, mid, up, above)


def days_kernel(fore_ref, obs_ref, fore_out, obs_out, error_out):
    slot = lax.axis_index("slot")
    for k in range(SLOTS):
        lead = lax.rem(slot + k, SLOTS)

        def step(d, squared):
            fore = fore_ref[d, lead].astype(jnp.float32).reshape(FLAT, DEST_MERIDIANS)
            obs = obs_ref[d, lead].astype(jnp.float32).reshape(FLAT, DEST_MERIDIANS)
            fore_out[k, d] = fore.astype(jnp.bfloat16)
            obs_out[k, d] = obs.astype(jnp.bfloat16)
            error = fore - obs
            return squared + error * error

        zero = jnp.zeros((FLAT, DEST_MERIDIANS), jnp.float32)
        error_out[k] = lax.fori_loop(0, DAYS, step, zero, unroll=2)


def relaid_days(fore, obs):
    vmem = pl.BlockSpec(memory_space=pltpu.VMEM)
    grid = jax.ShapeDtypeStruct((SLOTS, DAYS, FLAT, DEST_MERIDIANS), jnp.bfloat16)
    return pl.pallas_call(
        days_kernel,
        in_specs=[vmem] * 2,
        out_specs=[vmem] * 3,
        out_shape=[grid, grid, jax.ShapeDtypeStruct((SLOTS, FLAT, DEST_MERIDIANS), jnp.float32)],
        compiler_params=params(16),
        cost_estimate=cost(5),
        name="days",
    )(fore, obs)


def decode_kernel(own_ref, right_ref, left_ref, near_ref):
    near_ref[:BINS] = decode(own_ref[...])
    near_ref[BINS : 2 * BINS] = decode(right_ref[...])
    near_ref[2 * BINS :] = decode(left_ref[...])


def decoded(own, right, left):
    vmem = pl.BlockSpec(memory_space=pltpu.VMEM)
    return pl.pallas_call(
        decode_kernel,
        in_specs=[vmem] * 3,
        out_specs=vmem,
        out_shape=jax.ShapeDtypeStruct((3 * BINS, FLAT, DEST_MERIDIANS), jnp.float32),
        compiler_params=params(8),
        cost_estimate=cost(1),
        name="decode",
    )(own, right, left)


def lead_sums(k, bins_ref, near_ref, far_ref, fore_ref, obs_ref, error_ref, out_ref):
    slot = lax.axis_index("slot")
    lead = lax.rem(slot + k, SLOTS)
    half = FLAT // 2
    for h in range(2):
        some = slice(h * half, (h + 1) * half)

        def step(d, sums):
            cross, fore_sq, true_sq = sums
            wanted = bins_ref[lead, d]
            turn = (wanted // BINS - slot) % SLOTS
            place = wanted % BINS
            near = jnp.where(turn == 3, 2, jnp.minimum(turn, 1)) * BINS + place
            clim = jnp.where(turn == 2, far_ref[place, some], near_ref[near, some])
            fore_anom = fore_ref[k, d, some].astype(jnp.float32) - clim
            true_anom = obs_ref[k, d, some].astype(jnp.float32) - clim
            return (
                cross + fore_anom * true_anom,
                fore_sq + fore_anom * fore_anom,
                true_sq + true_anom * true_anom,
            )

        zero = jnp.zeros((half, DEST_MERIDIANS), jnp.float32)
        sums = lax.fori_loop(0, DAYS, step, (zero,) * 3, unroll=4)
        for n, value in enumerate(sums):
            out_ref[n + 1, some] = value
    out_ref[0] = error_ref[k]


def first_kernel(
    k, bins_ref, near_ref, low_ref, high_ref, fore_ref, obs_ref, error_ref, out_ref, far_ref
):
    far_ref[: BINS // 2] = decode(low_ref[...])
    far_ref[BINS // 2 :] = decode(high_ref[...])
    lead_sums(k, bins_ref, near_ref, far_ref, fore_ref, obs_ref, error_ref, out_ref)


def skill_sums(k, bins, near, far, fore, obs, error):
    vmem = pl.BlockSpec(memory_space=pltpu.VMEM)
    out = jax.ShapeDtypeStruct((4, FLAT, DEST_MERIDIANS), jnp.float32)
    clim = jax.ShapeDtypeStruct((BINS, FLAT, DEST_MERIDIANS), jnp.float32)
    first = len(far) == 2
    return pl.pallas_call(
        functools.partial(first_kernel if first else lead_sums, k),
        in_specs=[pl.BlockSpec(memory_space=pltpu.SMEM)] + [vmem] * (4 + len(far)),
        out_specs=[vmem, vmem] if first else vmem,
        out_shape=[out, clim] if first else out,
        compiler_params=params(16),
        cost_estimate=cost(1),
    )(bins, near, *far, fore, obs, error)


def maps_kernel(scale_ref, one_ref, two_ref, three_ref, own_ref, rmse_ref, acc_ref):
    lat = lax.axis_index("lat")
    total = own_ref[...] + one_ref[...] + two_ref[...] + three_ref[...]
    line = lax.broadcasted_iota(jnp.int32, (FLAT, DEST_MERIDIANS), 0)
    scale = jnp.zeros((FLAT, DEST_MERIDIANS), jnp.float32)
    for t in range(TILE):
        scale = jnp.where(line % TILE == t, scale_ref[lat * TILE + t], scale)
    days = DAYS * SLOTS
    rmse = jnp.sqrt(scale * total[0] / days)
    acc = total[1] / jnp.sqrt(total[2] * total[3] + 1e-06)
    rmse_ref[0] = rmse.reshape(VARS, TILE, DEST_MERIDIANS)
    acc_ref[0] = acc.reshape(VARS, TILE, DEST_MERIDIANS)


def maps(one, two, three, own):
    phi = (np.arange(DEST_PARALLELS, dtype=np.float32) + np.float32(0.5)) * np.float32(
        math.pi / DEST_PARALLELS
    ) - np.float32(0.5 * math.pi)
    cosine = np.cos(phi).astype(np.float32)
    scale = jnp.asarray(cosine / cosine.mean(dtype=np.float32))
    vmem = pl.BlockSpec(memory_space=pltpu.VMEM)
    shape = jax.ShapeDtypeStruct((1, VARS, TILE, DEST_MERIDIANS), jnp.float32)
    return pl.pallas_call(
        maps_kernel,
        in_specs=[pl.BlockSpec(memory_space=pltpu.SMEM)] + [vmem] * 4,
        out_specs=[vmem] * 2,
        out_shape=[shape] * 2,
        compiler_params=params(8),
        cost_estimate=cost(1),
        name="maps",
    )(scale, one, two, three, own)


def body(normals, index, extent, count, bins, prognosis, analysis):
    field = jnp.transpose(normals, (0, 2, 1, 3))
    table = lon_table()
    down, up = edges(field, table)
    devices = lax.axis_size("lat")
    below = lax.ppermute(up, "lat", [(i, i + 1) for i in range(devices - 1)])
    above = lax.ppermute(down, "lat", [(i + 1, i) for i in range(devices - 1)])
    mid = middle(field, table)
    own = climate_code(index, extent, count, below, down, mid, up, above)
    left = shifted(own, 1)
    right = shifted(own, -1)
    half = BINS // 2
    far_low = shifted(left[:half], 1)
    far_high = shifted(right[half:], -1)
    fore, obs, error = relaid_days(prognosis, analysis)
    near = decoded(own, right, left)
    wanted = jnp.transpose(bins)
    to_two, far = skill_sums(2, wanted, near, (far_low, far_high), fore, obs, error)
    two = shifted(to_two, 2)
    one = shifted(skill_sums(1, wanted, near, (far,), fore, obs, error), 1)
    three = shifted(skill_sums(3, wanted, near, (far,), fore, obs, error), 3)
    mine = skill_sums(0, wanted, near, (far,), fore, obs, error)
    return tuple(maps(one, two, three, mine))


def solution(mesh):
    placed = (
        P("slot", None, "lat", None),
        P("lat", None),
        P("lat", None),
        P("lat"),
        P("slot", None),
        P("slot", None, None, "lat", None),
        P("slot", None, None, "lat", None),
    )

    return jax.shard_map(
        body,
        mesh=mesh,
        in_specs=placed,
        out_specs=(P("slot", None, "lat", None), P("slot", None, "lat", None)),
        check_vma=False,
    )
```

```python
import functools
import math

import jax
import jax.numpy as jnp
import numpy as np
from jax import lax
from jax.experimental import pallas as pl
from jax.experimental.pallas import tpu as pltpu
from jax.sharding import PartitionSpec as P

SRC_LON = 1440
DEST_PARALLELS = 128
DEST_MERIDIANS = 240
FINE = SRC_LON // DEST_MERIDIANS
VARS = 8
BAND = 22
TILE = 4
OVER = 10
EDGE = 3
ROWS = BAND + 2 * EDGE
BINS = 16
HALF = BINS // 2
DAYS = 32
SLOTS = 4
FLAT = VARS * TILE
LON_LIMIT = 52
CODE_RATE = 10.0
CODE_BASE = 120.0


def shifted(value, step):
    slots = lax.axis_size("slot")
    return lax.ppermute(value, "slot", [(i, (i + step) % slots) for i in range(slots)])


def fill_table(table_ref):
    lines = 96
    line = lax.broadcasted_iota(jnp.int32, (lines, DEST_MERIDIANS), 0)
    start = FINE * lax.broadcasted_iota(jnp.int32, (lines, DEST_MERIDIANS), 1)
    for first in range(0, SRC_LON, lines):
        place = line + first - start
        inside = (place >= 0) & (place < FINE)
        table_ref[first : first + lines] = jnp.where(inside, 1.0, 0.0).astype(jnp.bfloat16)


def lon_mean(rows, table):
    flat = rows.reshape(-1, SRC_LON)
    total = jnp.dot(flat, table, preferred_element_type=jnp.float32)
    return (total * (1.0 / FINE)).astype(jnp.bfloat16).reshape(*rows.shape[:-1], DEST_MERIDIANS)


def params(mebibytes):
    return pltpu.CompilerParams(vmem_limit_bytes=mebibytes * 1024 * 1024)


def cost(microseconds):
    return pl.CostEstimate(
        flops=0, bytes_accessed=int(microseconds * 3 * 10**6), transcendentals=0
    )


def lon_kernel(field_ref, own_ref, cross_ref, inner_ref, buf, table_buf, sems):
    parts = sems.shape[0]
    size = BINS // parts
    odd = lax.rem(lax.axis_index("lat"), 2)
    cross_first = odd * (BAND - EDGE)
    inner_first = (1 - odd) * (BAND - EDGE)
    copies = []
    for n in range(parts):
        some = pl.ds(n * size, size)
        copy = pltpu.make_async_copy(field_ref.at[some], buf.at[some], sems.at[n])
        copy.start()
        copies.append(copy)
    fill_table(table_buf)
    for s in range(BINS):
        if s % size == 0:
            copies[s // size].wait()
        own_ref[s] = lon_mean(buf[s], table_buf[...])
        cross_ref[s] = own_ref[s, pl.ds(cross_first, EDGE)]
        inner_ref[s] = own_ref[s, pl.ds(inner_first, EDGE)]


def lon_rows(field):
    parts = 4
    hbm = pl.BlockSpec(memory_space=pl.ANY)
    vmem = pl.BlockSpec(memory_space=pltpu.VMEM)
    shape = lambda count: jax.ShapeDtypeStruct((BINS, count, VARS, DEST_MERIDIANS), jnp.bfloat16)
    return pl.pallas_call(
        lon_kernel,
        in_specs=[hbm],
        out_specs=[vmem] * 3,
        out_shape=[shape(BAND), shape(EDGE), shape(EDGE)],
        scratch_shapes=[
            pltpu.VMEM((BINS, BAND, VARS, SRC_LON), jnp.bfloat16),
            pltpu.VMEM((SRC_LON, DEST_MERIDIANS), jnp.bfloat16),
            pltpu.SemaphoreType.DMA((parts,)),
        ],
        compiler_params=params(LON_LIMIT),
        cost_estimate=cost(6),
        name="lon_rows",
    )(field)


def encode(value):
    size = jnp.exp2(CODE_RATE * jnp.abs(value) - CODE_BASE)
    return jnp.where(value < 0, -size, size).astype(jnp.bfloat16)


def decode(code):
    wide = code.astype(jnp.float32)
    size = (jnp.log2(jnp.abs(wide)) + CODE_BASE) * (1.0 / CODE_RATE)
    return jnp.where(wide < 0, -size, size)


def weight_matrix(index_ref, extent_ref, count_ref):
    lat = lax.axis_index("lat")
    odd = lax.rem(lat, 2) == 1
    line = lax.broadcasted_iota(jnp.int32, (FLAT, ROWS * VARS), 0)
    lane = lax.broadcasted_iota(jnp.int32, (FLAT, ROWS * VARS), 1)
    place = jnp.where(line // TILE == lane % VARS, lane // VARS, -1)
    dense = jnp.zeros((FLAT, ROWS * VARS), jnp.float32)
    sums = jnp.ones((FLAT, ROWS * VARS), jnp.float32)
    for t in range(TILE):
        here = line % TILE == t
        spot = jnp.where(here, place, -1)
        total = jnp.float32(0.0)
        for k in range(OVER):
            value = jnp.where(k < count_ref[t], extent_ref[t, k], jnp.float32(0.0))
            total = total + value
            row = index_ref[t, k] - lat * BAND
            beyond = jnp.where(row >= BAND, row - BAND - EDGE, row)
            turned = jnp.where(row < 0, row + BAND + EDGE, beyond)
            column = jnp.where(odd, turned, row) + EDGE
            dense = dense + jnp.where(spot == column, value, 0.0)
        sums = jnp.where(here, total, sums)
    dense = dense / sums
    high = dense.astype(jnp.bfloat16)
    rest = dense - high.astype(jnp.float32)
    middle_part = rest.astype(jnp.bfloat16)
    low = (rest - middle_part.astype(jnp.float32)).astype(jnp.bfloat16)
    return jnp.concatenate([high, middle_part, low], axis=0)


def climate_kernel(
    index_ref, extent_ref, count_ref, cross_ref, own_ref, inner_ref, low_ref, high_ref
):
    weights = weight_matrix(index_ref, extent_ref, count_ref)
    for s in range(BINS):
        rows = jnp.concatenate([cross_ref[s], own_ref[s], inner_ref[s]], axis=0)
        rows = rows.reshape(ROWS * VARS, DEST_MERIDIANS)
        parts = jnp.dot(weights, rows, preferred_element_type=jnp.float32)
        value = parts[:FLAT] + parts[FLAT : 2 * FLAT] + parts[2 * FLAT :]
        out_ref = low_ref if s < HALF else high_ref
        out_ref[s % HALF] = encode(value)


def climate_code(index, extent, count, cross, own, inner):
    smem = pl.BlockSpec(memory_space=pltpu.SMEM)
    vmem = pl.BlockSpec(memory_space=pltpu.VMEM)
    return pl.pallas_call(
        climate_kernel,
        in_specs=[smem] * 3 + [vmem] * 3,
        out_specs=[vmem] * 2,
        out_shape=[jax.ShapeDtypeStruct((HALF, FLAT, DEST_MERIDIANS), jnp.bfloat16)] * 2,
        compiler_params=params(8),
        cost_estimate=cost(2),
        name="climate",
    )(index, extent, count, cross, own, inner)


def days_kernel(fore_ref, obs_ref, fore_out, obs_out, error_out):
    slot = lax.axis_index("slot")
    for k in range(SLOTS):
        lead = lax.rem(slot + k, SLOTS)

        def step(d, squared):
            fore = fore_ref[d, lead].astype(jnp.float32).reshape(FLAT, DEST_MERIDIANS)
            obs = obs_ref[d, lead].astype(jnp.float32).reshape(FLAT, DEST_MERIDIANS)
            fore_out[k, d] = fore.astype(jnp.bfloat16)
            obs_out[k, d] = obs.astype(jnp.bfloat16)
            error = fore - obs
            return squared + error * error

        zero = jnp.zeros((FLAT, DEST_MERIDIANS), jnp.float32)
        error_out[k] = lax.fori_loop(0, DAYS, step, zero, unroll=2)


def relaid_days(fore, obs):
    vmem = pl.BlockSpec(memory_space=pltpu.VMEM)
    grid = jax.ShapeDtypeStruct((SLOTS, DAYS, FLAT, DEST_MERIDIANS), jnp.bfloat16)
    return pl.pallas_call(
        days_kernel,
        in_specs=[vmem] * 2,
        out_specs=[vmem] * 3,
        out_shape=[grid, grid, jax.ShapeDtypeStruct((SLOTS, FLAT, DEST_MERIDIANS), jnp.float32)],
        compiler_params=params(16),
        cost_estimate=cost(5),
        name="days",
    )(fore, obs)


def decode_kernel(*refs):
    near_ref = refs[-1]
    for n, code_ref in enumerate(refs[:-1]):
        near_ref[n * HALF : (n + 1) * HALF] = decode(code_ref[...])


def decoded(*codes):
    vmem = pl.BlockSpec(memory_space=pltpu.VMEM)
    return pl.pallas_call(
        decode_kernel,
        in_specs=[vmem] * len(codes),
        out_specs=vmem,
        out_shape=jax.ShapeDtypeStruct((len(codes) * HALF, FLAT, DEST_MERIDIANS), jnp.float32),
        compiler_params=params(8),
        cost_estimate=cost(1),
        name="decode",
    )(*codes)


def lead_sums(k, bins_ref, clim_ref, fore_ref, obs_ref, error_ref, out_ref):
    slot = lax.axis_index("slot")
    lead = lax.rem(slot + k, SLOTS)
    first = slot * BINS
    half = FLAT // 2
    for h in range(2):
        some = slice(h * half, (h + 1) * half)

        def step(d, sums):
            cross, fore_sq, true_sq = sums
            clim = clim_ref[(bins_ref[lead, d] - first) & (SLOTS * BINS - 1), some]
            fore_anom = fore_ref[k, d, some].astype(jnp.float32) - clim
            true_anom = obs_ref[k, d, some].astype(jnp.float32) - clim
            return (
                cross + fore_anom * true_anom,
                fore_sq + fore_anom * fore_anom,
                true_sq + true_anom * true_anom,
            )

        zero = jnp.zeros((half, DEST_MERIDIANS), jnp.float32)
        sums = lax.fori_loop(0, DAYS, step, (zero,) * 3, unroll=4)
        for n, value in enumerate(sums):
            out_ref[n + 1, some] = value
    out_ref[0] = error_ref[k]


def first_kernel(
    k, bins_ref, near_ref, low_ref, high_ref, fore_ref, obs_ref, error_ref, out_ref, clim_ref
):
    clim_ref[: 2 * BINS] = near_ref[: 2 * BINS]
    clim_ref[3 * BINS :] = near_ref[2 * BINS :]
    clim_ref[2 * BINS : 2 * BINS + HALF] = decode(low_ref[...])
    clim_ref[2 * BINS + HALF : 3 * BINS] = decode(high_ref[...])
    lead_sums(k, bins_ref, clim_ref, fore_ref, obs_ref, error_ref, out_ref)


def skill_sums(k, bins, clim, fore, obs, error):
    vmem = pl.BlockSpec(memory_space=pltpu.VMEM)
    out = jax.ShapeDtypeStruct((4, FLAT, DEST_MERIDIANS), jnp.float32)
    whole = jax.ShapeDtypeStruct((SLOTS * BINS, FLAT, DEST_MERIDIANS), jnp.float32)
    first = len(clim) > 1
    return pl.pallas_call(
        functools.partial(first_kernel if first else lead_sums, k),
        in_specs=[pl.BlockSpec(memory_space=pltpu.SMEM)] + [vmem] * (3 + len(clim)),
        out_specs=[vmem, vmem] if first else vmem,
        out_shape=[out, whole] if first else out,
        compiler_params=params(16),
        cost_estimate=cost(1),
    )(bins, *clim, fore, obs, error)


def maps_kernel(scale_ref, one_ref, two_ref, three_ref, own_ref, rmse_ref, acc_ref):
    lat = lax.axis_index("lat")
    total = own_ref[...] + one_ref[...] + two_ref[...] + three_ref[...]
    line = lax.broadcasted_iota(jnp.int32, (FLAT, DEST_MERIDIANS), 0)
    scale = jnp.zeros((FLAT, DEST_MERIDIANS), jnp.float32)
    for t in range(TILE):
        scale = jnp.where(line % TILE == t, scale_ref[lat * TILE + t], scale)
    days = DAYS * SLOTS
    rmse = jnp.sqrt(scale * total[0] / days)
    acc = total[1] / jnp.sqrt(total[2] * total[3] + 1e-06)
    rmse_ref[0] = rmse.reshape(VARS, TILE, DEST_MERIDIANS)
    acc_ref[0] = acc.reshape(VARS, TILE, DEST_MERIDIANS)


def maps(one, two, three, own):
    phi = (np.arange(DEST_PARALLELS, dtype=np.float32) + np.float32(0.5)) * np.float32(
        math.pi / DEST_PARALLELS
    ) - np.float32(0.5 * math.pi)
    cosine = np.cos(phi).astype(np.float32)
    scale = jnp.asarray(cosine / cosine.mean(dtype=np.float32))
    vmem = pl.BlockSpec(memory_space=pltpu.VMEM)
    shape = jax.ShapeDtypeStruct((1, VARS, TILE, DEST_MERIDIANS), jnp.float32)
    return pl.pallas_call(
        maps_kernel,
        in_specs=[pl.BlockSpec(memory_space=pltpu.SMEM)] + [vmem] * 4,
        out_specs=[vmem] * 2,
        out_shape=[shape] * 2,
        compiler_params=params(8),
        cost_estimate=cost(1),
        name="maps",
    )(scale, one, two, three, own)


def body(normals, index, extent, count, bins, prognosis, analysis):
    field = jnp.transpose(normals, (0, 2, 1, 3))
    own, cross_edge, inner_edge = lon_rows(field)
    devices = lax.axis_size("lat")
    meets = [(i, i + 1) for i in range(1, devices - 1, 2)]
    meets += [(j, i) for i, j in meets]
    cross = lax.ppermute(cross_edge, "lat", meets)
    inner = lax.ppermute(inner_edge, "lat", [(i, i ^ 1) for i in range(devices)])
    fore, obs, error = relaid_days(prognosis, analysis)
    low, high = climate_code(index, extent, count, cross, own, inner)
    left_low = shifted(low, 1)
    right_high = shifted(high, -1)
    left_high = shifted(high, 1)
    right_low = shifted(low, -1)
    far_low = shifted(left_low, 1)
    far_high = shifted(right_high, -1)
    near = decoded(low, high, right_low, right_high, left_low, left_high)
    wanted = jnp.transpose(bins)
    to_two, clim = skill_sums(2, wanted, (near, far_low, far_high), fore, obs, error)
    two = shifted(to_two, 2)
    one = shifted(skill_sums(1, wanted, (clim,), fore, obs, error), 1)
    three = shifted(skill_sums(3, wanted, (clim,), fore, obs, error), 3)
    mine = skill_sums(0, wanted, (clim,), fore, obs, error)
    return tuple(maps(one, two, three, mine))


def solution(mesh):
    placed = (
        P("slot", None, "lat", None),
        P("lat", None),
        P("lat", None),
        P("lat"),
        P("slot", None),
        P("slot", None, None, "lat", None),
        P("slot", None, None, "lat", None),
    )

    return jax.shard_map(
        body,
        mesh=mesh,
        in_specs=placed,
        out_specs=(P("slot", None, "lat", None), P("slot", None, "lat", None)),
        check_vma=False,
    )
```

```python
import math

import jax
import jax.numpy as jnp
import numpy as np
from jax import lax
from jax.experimental import pallas as pl
from jax.experimental.pallas import tpu as pltpu
from jax.sharding import PartitionSpec as P

SRC_LON = 1440
DEST_PARALLELS = 128
DEST_MERIDIANS = 240
FINE = SRC_LON // DEST_MERIDIANS
VARS = 8
BAND = 22
TILE = 4
OVER = 10
EDGE = 3
MID = BAND - 2 * EDGE
ROWS = BAND + 2 * EDGE
SPAN = BAND + EDGE
BINS = 16
HALF = BINS // 2
DAYS = 32
SLOTS = 4
FLAT = VARS * TILE
EDGE_LIMIT = 57
MID_LIMIT = 50
CODE_RATE = 10.0
CODE_BASE = 120.0
SUM_SCALE = 64.0
SUM_FLOOR = 2.0**-126


def shifted(value, step):
    slots = lax.axis_size("slot")
    return lax.ppermute(value, "slot", [(i, (i + step) % slots) for i in range(slots)])


def fill_table(table_ref):
    lines = 96
    line = lax.broadcasted_iota(jnp.int32, (lines, DEST_MERIDIANS), 0)
    start = FINE * lax.broadcasted_iota(jnp.int32, (lines, DEST_MERIDIANS), 1)
    for first in range(0, SRC_LON, lines):
        place = line + first - start
        inside = (place >= 0) & (place < FINE)
        table_ref[first : first + lines] = jnp.where(inside, 1.0, 0.0).astype(jnp.bfloat16)


def lon_mean(rows, table):
    flat = rows.reshape(-1, SRC_LON)
    total = jnp.dot(flat, table, preferred_element_type=jnp.float32)
    return (total * (1.0 / FINE)).astype(jnp.bfloat16).reshape(*rows.shape[:-1], DEST_MERIDIANS)


def params(mebibytes):
    return pltpu.CompilerParams(vmem_limit_bytes=mebibytes * 1024 * 1024)


def cost(microseconds):
    return pl.CostEstimate(
        flops=0, bytes_accessed=int(microseconds * 3 * 10**6), transcendentals=0
    )


def edge_kernel(field_ref, cross_ref, inner_ref, buf, table_buf, sems):
    odd = lax.rem(lax.axis_index("lat"), 2)
    firsts = (odd * (BAND - EDGE), (1 - odd) * (BAND - EDGE))
    outs = (cross_ref, inner_ref)
    jobs = []
    for n, first in enumerate(firsts):
        for part in range(2):
            some = pl.ds(part * HALF, HALF)
            copy = pltpu.make_async_copy(
                field_ref.at[some, pl.ds(first, EDGE)], buf.at[n, some], sems.at[2 * n + part]
            )
            copy.start()
            jobs.append((copy, n, slice(part * HALF, (part + 1) * HALF)))
    fill_table(table_buf)
    for copy, n, some in jobs:
        copy.wait()
        outs[n][some] = lon_mean(buf[n, some], table_buf[...])


def edge_rows(field):
    vmem = pl.BlockSpec(memory_space=pltpu.VMEM)
    return pl.pallas_call(
        edge_kernel,
        in_specs=[pl.BlockSpec(memory_space=pl.ANY)],
        out_specs=[vmem] * 2,
        out_shape=[jax.ShapeDtypeStruct((BINS, EDGE, VARS, DEST_MERIDIANS), jnp.bfloat16)] * 2,
        scratch_shapes=[
            pltpu.VMEM((2, BINS, EDGE, VARS, SRC_LON), jnp.bfloat16),
            pltpu.VMEM((SRC_LON, DEST_MERIDIANS), jnp.bfloat16),
            pltpu.SemaphoreType.DMA((4,)),
        ],
        compiler_params=params(EDGE_LIMIT),
        cost_estimate=cost(2),
        name="edge_rows",
    )(field)


def mid_kernel(field_ref, out_ref, buf, table_buf, sems):
    parts = sems.shape[0]
    size = BINS // parts
    block = 2
    copies = []
    for n in range(parts):
        some = pl.ds(n * size, size)
        copy = pltpu.make_async_copy(
            field_ref.at[some, pl.ds(EDGE, MID)], buf.at[some], sems.at[n]
        )
        copy.start()
        copies.append(copy)
    fill_table(table_buf)
    for first in range(0, BINS, block):
        if first % size == 0:
            copies[first // size].wait()
        some = slice(first, first + block)
        out_ref[some] = lon_mean(buf[some], table_buf[...])


def mid_rows(field):
    parts = 4
    return pl.pallas_call(
        mid_kernel,
        in_specs=[pl.BlockSpec(memory_space=pl.ANY)],
        out_specs=pl.BlockSpec(memory_space=pltpu.VMEM),
        out_shape=jax.ShapeDtypeStruct((BINS, MID, VARS, DEST_MERIDIANS), jnp.bfloat16),
        scratch_shapes=[
            pltpu.VMEM((BINS, MID, VARS, SRC_LON), jnp.bfloat16),
            pltpu.VMEM((SRC_LON, DEST_MERIDIANS), jnp.bfloat16),
            pltpu.SemaphoreType.DMA((parts,)),
        ],
        compiler_params=params(MID_LIMIT),
        cost_estimate=cost(4),
        name="mid_rows",
    )(field)


def encode(value):
    size = jnp.exp2(CODE_RATE * jnp.abs(value) - CODE_BASE)
    return jnp.where(value < 0, -size, size).astype(jnp.bfloat16)


def decode(code):
    wide = code.astype(jnp.float32)
    size = (jnp.log2(jnp.abs(wide)) + CODE_BASE) * (1.0 / CODE_RATE)
    return jnp.where(wide < 0, -size, size)


def weight_matrix(index_ref, extent_ref, count_ref):
    lat = lax.axis_index("lat")
    odd = lax.rem(lat, 2) == 1
    line = lax.broadcasted_iota(jnp.int32, (FLAT, ROWS * VARS), 0)
    lane = lax.broadcasted_iota(jnp.int32, (FLAT, ROWS * VARS), 1)
    place = jnp.where(line // TILE == lane % VARS, lane // VARS, -1)
    dense = jnp.zeros((FLAT, ROWS * VARS), jnp.float32)
    sums = jnp.ones((FLAT, ROWS * VARS), jnp.float32)
    for t in range(TILE):
        here = line % TILE == t
        spot = jnp.where(here, place, -1)
        total = jnp.float32(0.0)
        for k in range(OVER):
            value = jnp.where(k < count_ref[t], extent_ref[t, k], jnp.float32(0.0))
            total = total + value
            row = index_ref[t, k] - lat * BAND
            inside = (row >= EDGE) & (row < BAND - EDGE)
            shift = jnp.where(inside, 0, jnp.where(row < 0, SPAN, -SPAN))
            shift = jnp.where((row >= 0) & (row < EDGE), BAND - EDGE, shift)
            shift = jnp.where((row >= BAND - EDGE) & (row < BAND), EDGE - BAND, shift)
            column = row + EDGE + jnp.where(odd, shift, 0)
            dense = dense + jnp.where(spot == column, value, 0.0)
        sums = jnp.where(here, total, sums)
    dense = dense / sums
    high = dense.astype(jnp.bfloat16)
    rest = dense - high.astype(jnp.float32)
    middle_part = rest.astype(jnp.bfloat16)
    low = (rest - middle_part.astype(jnp.float32)).astype(jnp.bfloat16)
    return jnp.concatenate([high, middle_part, low], axis=0)


def climate_kernel(
    index_ref, extent_ref, count_ref, cross_ref, cross_own, mid_ref, inner_own, inner_ref,
    low_ref, high_ref,
):
    weights = weight_matrix(index_ref, extent_ref, count_ref)
    for s in range(BINS):
        parts = (cross_ref, cross_own, mid_ref, inner_own, inner_ref)
        rows = jnp.concatenate([ref[s] for ref in parts], axis=0)
        rows = rows.reshape(ROWS * VARS, DEST_MERIDIANS)
        parts = jnp.dot(weights, rows, preferred_element_type=jnp.float32)
        value = parts[:FLAT] + parts[FLAT : 2 * FLAT] + parts[2 * FLAT :]
        out_ref = low_ref if s < HALF else high_ref
        out_ref[s % HALF] = encode(value)


def climate_code(*arrays):
    smem = pl.BlockSpec(memory_space=pltpu.SMEM)
    vmem = pl.BlockSpec(memory_space=pltpu.VMEM)
    return pl.pallas_call(
        climate_kernel,
        in_specs=[smem] * 3 + [vmem] * 5,
        out_specs=[vmem] * 2,
        out_shape=[jax.ShapeDtypeStruct((HALF, FLAT, DEST_MERIDIANS), jnp.bfloat16)] * 2,
        compiler_params=params(8),
        cost_estimate=cost(2),
        name="climate",
    )(*arrays)


def days_kernel(fore_ref, obs_ref, fore_out, obs_out, error_out):
    slot = lax.axis_index("slot")
    for k in range(SLOTS):
        lead = lax.rem(slot + k, SLOTS)

        def step(d, squared):
            fore = fore_ref[d, lead].astype(jnp.float32).reshape(FLAT, DEST_MERIDIANS)
            obs = obs_ref[d, lead].astype(jnp.float32).reshape(FLAT, DEST_MERIDIANS)
            fore_out[k, d] = fore.astype(jnp.bfloat16)
            obs_out[k, d] = obs.astype(jnp.bfloat16)
            error = fore - obs
            return squared + error * error

        zero = jnp.zeros((FLAT, DEST_MERIDIANS), jnp.float32)
        error_out[k] = lax.fori_loop(0, DAYS, step, zero, unroll=2)


def relaid_days(fore, obs):
    vmem = pl.BlockSpec(memory_space=pltpu.VMEM)
    grid = jax.ShapeDtypeStruct((SLOTS, DAYS, FLAT, DEST_MERIDIANS), jnp.bfloat16)
    return pl.pallas_call(
        days_kernel,
        in_specs=[vmem] * 2,
        out_specs=[vmem] * 3,
        out_shape=[grid, grid, jax.ShapeDtypeStruct((SLOTS, FLAT, DEST_MERIDIANS), jnp.float32)],
        compiler_params=params(16),
        cost_estimate=cost(5),
        name="days",
    )(fore, obs)


def decode_kernel(*refs):
    near_ref = refs[-1]
    for n, code_ref in enumerate(refs[:-1]):
        near_ref[n * HALF : (n + 1) * HALF] = decode(code_ref[...])


def decoded(*codes):
    vmem = pl.BlockSpec(memory_space=pltpu.VMEM)
    return pl.pallas_call(
        decode_kernel,
        in_specs=[vmem] * len(codes),
        out_specs=vmem,
        out_shape=jax.ShapeDtypeStruct((len(codes) * HALF, FLAT, DEST_MERIDIANS), jnp.float32),
        compiler_params=params(8),
        cost_estimate=cost(1),
        name="decode",
    )(*codes)


def encode_sum(value):
    scaled = value * SUM_SCALE
    square = scaled * scaled
    power = square * square * square
    return jnp.where(value < 0, -power, power).astype(jnp.bfloat16)


def decode_sum(code):
    wide = code.astype(jnp.float32)
    size = jnp.maximum(jnp.abs(wide), SUM_FLOOR)
    root = jnp.exp2(jnp.log2(size) * (1.0 / 6.0)) * (1.0 / SUM_SCALE)
    return jnp.where(wide < 0, -root, root)


def lead_sums(k, bins_ref, clim_ref, fore_ref, obs_ref, error_ref, out_ref, kept):
    slot = lax.axis_index("slot")
    lead = lax.rem(slot + k, SLOTS)
    first = slot * BINS
    half = FLAT // 2
    for h in range(2):
        some = slice(h * half, (h + 1) * half)

        def step(d, sums):
            cross, fore_sq, true_sq = sums
            clim = clim_ref[(bins_ref[lead, d] - first) & (SLOTS * BINS - 1), some]
            fore_anom = fore_ref[k, d, some].astype(jnp.float32) - clim
            true_anom = obs_ref[k, d, some].astype(jnp.float32) - clim
            return (
                cross + fore_anom * true_anom,
                fore_sq + fore_anom * fore_anom,
                true_sq + true_anom * true_anom,
            )

        zero = jnp.zeros((half, DEST_MERIDIANS), jnp.float32)
        sums = lax.fori_loop(0, DAYS, step, (zero,) * 3, unroll=4)
        for n, value in enumerate(sums):
            out_ref[n + 1, some] = kept(value)
    out_ref[0] = kept(error_ref[k])


def others_kernel(
    bins_ref, near_ref, low_ref, high_ref, fore_ref, obs_ref, error_ref,
    one_ref, two_ref, three_ref, clim_ref,
):
    clim_ref[: 2 * BINS] = near_ref[: 2 * BINS]
    clim_ref[3 * BINS :] = near_ref[2 * BINS :]
    clim_ref[2 * BINS : 2 * BINS + HALF] = decode(low_ref[...])
    clim_ref[2 * BINS + HALF : 3 * BINS] = decode(high_ref[...])
    for k, out_ref in ((1, one_ref), (2, two_ref), (3, three_ref)):
        lead_sums(k, bins_ref, clim_ref, fore_ref, obs_ref, error_ref, out_ref, encode_sum)


def mine_kernel(bins_ref, clim_ref, fore_ref, obs_ref, error_ref, out_ref):
    lead_sums(0, bins_ref, clim_ref, fore_ref, obs_ref, error_ref, out_ref, lambda value: value)


def other_sums(bins, near, low, high, fore, obs, error):
    vmem = pl.BlockSpec(memory_space=pltpu.VMEM)
    code = jax.ShapeDtypeStruct((4, FLAT, DEST_MERIDIANS), jnp.bfloat16)
    whole = jax.ShapeDtypeStruct((SLOTS * BINS, FLAT, DEST_MERIDIANS), jnp.float32)
    return pl.pallas_call(
        others_kernel,
        in_specs=[pl.BlockSpec(memory_space=pltpu.SMEM)] + [vmem] * 6,
        out_specs=[vmem] * 4,
        out_shape=[code, code, code, whole],
        compiler_params=params(16),
        cost_estimate=cost(3),
        name="other_sums",
    )(bins, near, low, high, fore, obs, error)


def my_sums(bins, clim, fore, obs, error):
    vmem = pl.BlockSpec(memory_space=pltpu.VMEM)
    return pl.pallas_call(
        mine_kernel,
        in_specs=[pl.BlockSpec(memory_space=pltpu.SMEM)] + [vmem] * 4,
        out_specs=vmem,
        out_shape=jax.ShapeDtypeStruct((4, FLAT, DEST_MERIDIANS), jnp.float32),
        compiler_params=params(16),
        cost_estimate=cost(1),
        name="my_sums",
    )(bins, clim, fore, obs, error)


def maps_kernel(scale_ref, one_ref, two_ref, three_ref, own_ref, rmse_ref, acc_ref):
    lat = lax.axis_index("lat")
    total = own_ref[...]
    for code_ref in (one_ref, two_ref, three_ref):
        total = total + decode_sum(code_ref[...])
    line = lax.broadcasted_iota(jnp.int32, (FLAT, DEST_MERIDIANS), 0)
    scale = jnp.zeros((FLAT, DEST_MERIDIANS), jnp.float32)
    for t in range(TILE):
        scale = jnp.where(line % TILE == t, scale_ref[lat * TILE + t], scale)
    days = DAYS * SLOTS
    rmse = jnp.sqrt(scale * total[0] / days)
    acc = total[1] / jnp.sqrt(total[2] * total[3] + 1e-06)
    rmse_ref[0] = rmse.reshape(VARS, TILE, DEST_MERIDIANS)
    acc_ref[0] = acc.reshape(VARS, TILE, DEST_MERIDIANS)


def maps(one, two, three, own):
    phi = (np.arange(DEST_PARALLELS, dtype=np.float32) + np.float32(0.5)) * np.float32(
        math.pi / DEST_PARALLELS
    ) - np.float32(0.5 * math.pi)
    cosine = np.cos(phi).astype(np.float32)
    scale = jnp.asarray(cosine / cosine.mean(dtype=np.float32))
    vmem = pl.BlockSpec(memory_space=pltpu.VMEM)
    shape = jax.ShapeDtypeStruct((1, VARS, TILE, DEST_MERIDIANS), jnp.float32)
    return pl.pallas_call(
        maps_kernel,
        in_specs=[pl.BlockSpec(memory_space=pltpu.SMEM)] + [vmem] * 4,
        out_specs=[vmem] * 2,
        out_shape=[shape] * 2,
        compiler_params=params(8),
        cost_estimate=cost(1),
        name="maps",
    )(scale, one, two, three, own)


def body(normals, index, extent, count, bins, prognosis, analysis):
    field = jnp.transpose(normals, (0, 2, 1, 3))
    cross_own, inner_own = edge_rows(field)
    devices = lax.axis_size("lat")
    meets = [(i, i + 1) for i in range(1, devices - 1, 2)]
    meets += [(j, i) for i, j in meets]
    cross = lax.ppermute(cross_own, "lat", meets)
    inner = lax.ppermute(inner_own, "lat", [(i, i ^ 1) for i in range(devices)])
    mid = mid_rows(field)
    low, high = climate_code(index, extent, count, cross, cross_own, mid, inner_own, inner)
    left_low = shifted(low, 1)
    right_high = shifted(high, -1)
    left_high = shifted(high, 1)
    right_low = shifted(low, -1)
    far_low = shifted(left_low, 1)
    far_high = shifted(right_high, -1)
    fore, obs, error = relaid_days(prognosis, analysis)
    near = decoded(low, high, right_low, right_high, left_low, left_high)
    wanted = jnp.transpose(bins)
    to_one, to_two, to_three, clim = other_sums(
        wanted, near, far_low, far_high, fore, obs, error
    )
    two = shifted(to_two, 2)
    one = shifted(to_one, 1)
    three = shifted(to_three, 3)
    mine = my_sums(wanted, clim, fore, obs, error)
    return tuple(maps(one, two, three, mine))


def solution(mesh):
    placed = (
        P("slot", None, "lat", None),
        P("lat", None),
        P("lat", None),
        P("lat"),
        P("slot", None),
        P("slot", None, None, "lat", None),
        P("slot", None, None, "lat", None),
    )

    return jax.shard_map(
        body,
        mesh=mesh,
        in_specs=placed,
        out_specs=(P("slot", None, "lat", None), P("slot", None, "lat", None)),
        check_vma=False,
    )
```

```python
import math

import jax
import jax.numpy as jnp
import numpy as np
from jax import lax
from jax.experimental import pallas as pl
from jax.experimental.pallas import tpu as pltpu
from jax.sharding import PartitionSpec as P

SRC_LON = 1440
DEST_PARALLELS = 128
DEST_MERIDIANS = 240
FINE = SRC_LON // DEST_MERIDIANS
VARS = 8
BAND = 22
TILE = 4
OVER = 10
EDGE = 3
ROWS = BAND + 2 * EDGE
BINS = 16
HALF = BINS // 2
DAYS = 32
SLOTS = 4
FLAT = VARS * TILE
LON_LIMIT = 52
CODE_RATE = 10.0
CODE_BASE = 120.0
SUM_SCALE = 64.0
SUM_FLOOR = 2.0**-126


def shifted(value, step):
    slots = lax.axis_size("slot")
    return lax.ppermute(value, "slot", [(i, (i + step) % slots) for i in range(slots)])


def fill_table(table_ref):
    lines = 96
    line = lax.broadcasted_iota(jnp.int32, (lines, DEST_MERIDIANS), 0)
    start = FINE * lax.broadcasted_iota(jnp.int32, (lines, DEST_MERIDIANS), 1)
    for first in range(0, SRC_LON, lines):
        place = line + first - start
        inside = (place >= 0) & (place < FINE)
        table_ref[first : first + lines] = jnp.where(inside, 1.0, 0.0).astype(jnp.bfloat16)


def lon_mean(rows, table):
    flat = rows.reshape(-1, SRC_LON)
    total = jnp.dot(flat, table, preferred_element_type=jnp.float32)
    return (total * (1.0 / FINE)).astype(jnp.bfloat16).reshape(*rows.shape[:-1], DEST_MERIDIANS)


def params(mebibytes):
    return pltpu.CompilerParams(vmem_limit_bytes=mebibytes * 1024 * 1024)


def cost(microseconds):
    return pl.CostEstimate(
        flops=0, bytes_accessed=int(microseconds * 3 * 10**6), transcendentals=0
    )


def lon_kernel(field_ref, own_ref, cross_ref, inner_ref, buf, table_buf, sems):
    parts = sems.shape[0]
    size = BINS // parts
    odd = lax.rem(lax.axis_index("lat"), 2)
    cross_first = odd * (BAND - EDGE)
    inner_first = (1 - odd) * (BAND - EDGE)
    copies = []
    for n in range(parts):
        some = pl.ds(n * size, size)
        copy = pltpu.make_async_copy(field_ref.at[some], buf.at[some], sems.at[n])
        copy.start()
        copies.append(copy)
    fill_table(table_buf)
    for s in range(BINS):
        if s % size == 0:
            copies[s // size].wait()
        own_ref[s] = lon_mean(buf[s], table_buf[...])
        cross_ref[s] = own_ref[s, pl.ds(cross_first, EDGE)]
        inner_ref[s] = own_ref[s, pl.ds(inner_first, EDGE)]


def lon_rows(field):
    parts = 4
    hbm = pl.BlockSpec(memory_space=pl.ANY)
    vmem = pl.BlockSpec(memory_space=pltpu.VMEM)
    shape = lambda count: jax.ShapeDtypeStruct((BINS, count, VARS, DEST_MERIDIANS), jnp.bfloat16)
    return pl.pallas_call(
        lon_kernel,
        in_specs=[hbm],
        out_specs=[vmem] * 3,
        out_shape=[shape(BAND), shape(EDGE), shape(EDGE)],
        scratch_shapes=[
            pltpu.VMEM((BINS, BAND, VARS, SRC_LON), jnp.bfloat16),
            pltpu.VMEM((SRC_LON, DEST_MERIDIANS), jnp.bfloat16),
            pltpu.SemaphoreType.DMA((parts,)),
        ],
        compiler_params=params(LON_LIMIT),
        cost_estimate=cost(6),
        name="lon_rows",
    )(field)


def encode(value):
    size = jnp.exp2(CODE_RATE * jnp.abs(value) - CODE_BASE)
    return jnp.where(value < 0, -size, size).astype(jnp.bfloat16)


def decode(code):
    wide = code.astype(jnp.float32)
    size = (jnp.log2(jnp.abs(wide)) + CODE_BASE) * (1.0 / CODE_RATE)
    return jnp.where(wide < 0, -size, size)


def weight_matrix(index_ref, extent_ref, count_ref):
    lat = lax.axis_index("lat")
    odd = lax.rem(lat, 2) == 1
    line = lax.broadcasted_iota(jnp.int32, (FLAT, ROWS * VARS), 0)
    lane = lax.broadcasted_iota(jnp.int32, (FLAT, ROWS * VARS), 1)
    place = jnp.where(line // TILE == lane % VARS, lane // VARS, -1)
    dense = jnp.zeros((FLAT, ROWS * VARS), jnp.float32)
    sums = jnp.ones((FLAT, ROWS * VARS), jnp.float32)
    for t in range(TILE):
        here = line % TILE == t
        spot = jnp.where(here, place, -1)
        total = jnp.float32(0.0)
        for k in range(OVER):
            value = jnp.where(k < count_ref[t], extent_ref[t, k], jnp.float32(0.0))
            total = total + value
            row = index_ref[t, k] - lat * BAND
            beyond = jnp.where(row >= BAND, row - BAND - EDGE, row)
            turned = jnp.where(row < 0, row + BAND + EDGE, beyond)
            column = jnp.where(odd, turned, row) + EDGE
            dense = dense + jnp.where(spot == column, value, 0.0)
        sums = jnp.where(here, total, sums)
    dense = dense / sums
    high = dense.astype(jnp.bfloat16)
    rest = dense - high.astype(jnp.float32)
    middle_part = rest.astype(jnp.bfloat16)
    low = (rest - middle_part.astype(jnp.float32)).astype(jnp.bfloat16)
    return jnp.concatenate([high, middle_part, low], axis=0)


def climate_kernel(weights_ref, cross_ref, own_ref, inner_ref, low_ref, high_ref):
    weights = weights_ref[...]
    for s in range(BINS):
        rows = jnp.concatenate([cross_ref[s], own_ref[s], inner_ref[s]], axis=0)
        rows = rows.reshape(ROWS * VARS, DEST_MERIDIANS)
        parts = jnp.dot(weights, rows, preferred_element_type=jnp.float32)
        value = parts[:FLAT] + parts[FLAT : 2 * FLAT] + parts[2 * FLAT :]
        out_ref = low_ref if s < HALF else high_ref
        out_ref[s % HALF] = encode(value)


def climate_code(*arrays):
    vmem = pl.BlockSpec(memory_space=pltpu.VMEM)
    return pl.pallas_call(
        climate_kernel,
        in_specs=[vmem] * 4,
        out_specs=[vmem] * 2,
        out_shape=[jax.ShapeDtypeStruct((HALF, FLAT, DEST_MERIDIANS), jnp.bfloat16)] * 2,
        compiler_params=params(8),
        cost_estimate=cost(2),
        name="climate",
    )(*arrays)


def days_kernel(
    index_ref, extent_ref, count_ref, fore_ref, obs_ref, fore_out, obs_out, error_out, weights_out
):
    weights_out[...] = weight_matrix(index_ref, extent_ref, count_ref)
    slot = lax.axis_index("slot")
    for k in range(SLOTS):
        lead = lax.rem(slot + k, SLOTS)

        def step(d, squared):
            fore = fore_ref[d, lead].astype(jnp.float32).reshape(FLAT, DEST_MERIDIANS)
            obs = obs_ref[d, lead].astype(jnp.float32).reshape(FLAT, DEST_MERIDIANS)
            fore_out[k, d] = fore.astype(jnp.bfloat16)
            obs_out[k, d] = obs.astype(jnp.bfloat16)
            error = fore - obs
            return squared + error * error

        zero = jnp.zeros((FLAT, DEST_MERIDIANS), jnp.float32)
        error_out[k] = lax.fori_loop(0, DAYS, step, zero, unroll=2)


def relaid_days(index, extent, count, fore, obs):
    smem = pl.BlockSpec(memory_space=pltpu.SMEM)
    vmem = pl.BlockSpec(memory_space=pltpu.VMEM)
    grid = jax.ShapeDtypeStruct((SLOTS, DAYS, FLAT, DEST_MERIDIANS), jnp.bfloat16)
    error = jax.ShapeDtypeStruct((SLOTS, FLAT, DEST_MERIDIANS), jnp.float32)
    weights = jax.ShapeDtypeStruct((3 * FLAT, ROWS * VARS), jnp.bfloat16)
    return pl.pallas_call(
        days_kernel,
        in_specs=[smem] * 3 + [vmem] * 2,
        out_specs=[vmem] * 4,
        out_shape=[grid, grid, error, weights],
        compiler_params=params(16),
        cost_estimate=cost(2),
        name="days",
    )(index, extent, count, fore, obs)


def decode_kernel(*refs):
    near_ref = refs[-1]
    for n, code_ref in enumerate(refs[:-1]):
        near_ref[n * HALF : (n + 1) * HALF] = decode(code_ref[...])


def decoded(*codes):
    vmem = pl.BlockSpec(memory_space=pltpu.VMEM)
    return pl.pallas_call(
        decode_kernel,
        in_specs=[vmem] * len(codes),
        out_specs=vmem,
        out_shape=jax.ShapeDtypeStruct((len(codes) * HALF, FLAT, DEST_MERIDIANS), jnp.float32),
        compiler_params=params(8),
        cost_estimate=cost(1),
        name="decode",
    )(*codes)


def encode_sum(value):
    scaled = value * SUM_SCALE
    square = scaled * scaled
    power = square * square * square
    return jnp.where(value < 0, -power, power).astype(jnp.bfloat16)


def decode_sum(code):
    wide = code.astype(jnp.float32)
    size = jnp.maximum(jnp.abs(wide), SUM_FLOOR)
    root = jnp.exp2(jnp.log2(size) * (1.0 / 6.0)) * (1.0 / SUM_SCALE)
    return jnp.where(wide < 0, -root, root)


def lead_sums(k, bins_ref, clim_ref, fore_ref, obs_ref, error_ref, out_ref, kept):
    slot = lax.axis_index("slot")
    lead = lax.rem(slot + k, SLOTS)
    first = slot * BINS
    half = FLAT // 2
    for h in range(2):
        some = slice(h * half, (h + 1) * half)

        def step(d, sums):
            cross, fore_sq, true_sq = sums
            clim = clim_ref[(bins_ref[lead, d] - first) & (SLOTS * BINS - 1), some]
            fore_anom = fore_ref[k, d, some].astype(jnp.float32) - clim
            true_anom = obs_ref[k, d, some].astype(jnp.float32) - clim
            return (
                cross + fore_anom * true_anom,
                fore_sq + fore_anom * fore_anom,
                true_sq + true_anom * true_anom,
            )

        zero = jnp.zeros((half, DEST_MERIDIANS), jnp.float32)
        sums = lax.fori_loop(0, DAYS, step, (zero,) * 3, unroll=8)
        for n, value in enumerate(sums):
            out_ref[n + 1, some] = kept(value)
    out_ref[0] = kept(error_ref[k])


def others_kernel(
    bins_ref, near_ref, low_ref, high_ref, fore_ref, obs_ref, error_ref,
    one_ref, two_ref, three_ref, clim_ref,
):
    clim_ref[: 2 * BINS] = near_ref[: 2 * BINS]
    clim_ref[3 * BINS :] = near_ref[2 * BINS :]
    clim_ref[2 * BINS : 2 * BINS + HALF] = decode(low_ref[...])
    clim_ref[2 * BINS + HALF : 3 * BINS] = decode(high_ref[...])
    for k, out_ref in ((1, one_ref), (2, two_ref), (3, three_ref)):
        lead_sums(k, bins_ref, clim_ref, fore_ref, obs_ref, error_ref, out_ref, encode_sum)


def mine_kernel(bins_ref, clim_ref, fore_ref, obs_ref, error_ref, out_ref):
    lead_sums(0, bins_ref, clim_ref, fore_ref, obs_ref, error_ref, out_ref, lambda value: value)


def other_sums(bins, near, low, high, fore, obs, error):
    vmem = pl.BlockSpec(memory_space=pltpu.VMEM)
    code = jax.ShapeDtypeStruct((4, FLAT, DEST_MERIDIANS), jnp.bfloat16)
    whole = jax.ShapeDtypeStruct((SLOTS * BINS, FLAT, DEST_MERIDIANS), jnp.float32)
    return pl.pallas_call(
        others_kernel,
        in_specs=[pl.BlockSpec(memory_space=pltpu.SMEM)] + [vmem] * 6,
        out_specs=[vmem] * 4,
        out_shape=[code, code, code, whole],
        compiler_params=params(16),
        cost_estimate=cost(3),
        name="other_sums",
    )(bins, near, low, high, fore, obs, error)


def my_sums(bins, clim, fore, obs, error):
    vmem = pl.BlockSpec(memory_space=pltpu.VMEM)
    return pl.pallas_call(
        mine_kernel,
        in_specs=[pl.BlockSpec(memory_space=pltpu.SMEM)] + [vmem] * 4,
        out_specs=vmem,
        out_shape=jax.ShapeDtypeStruct((4, FLAT, DEST_MERIDIANS), jnp.float32),
        compiler_params=params(16),
        cost_estimate=cost(1),
        name="my_sums",
    )(bins, clim, fore, obs, error)


def maps_kernel(scale_ref, one_ref, two_ref, three_ref, own_ref, rmse_ref, acc_ref):
    lat = lax.axis_index("lat")
    total = own_ref[...]
    for code_ref in (one_ref, two_ref, three_ref):
        total = total + decode_sum(code_ref[...])
    line = lax.broadcasted_iota(jnp.int32, (FLAT, DEST_MERIDIANS), 0)
    scale = jnp.zeros((FLAT, DEST_MERIDIANS), jnp.float32)
    for t in range(TILE):
        scale = jnp.where(line % TILE == t, scale_ref[lat * TILE + t], scale)
    days = DAYS * SLOTS
    rmse = jnp.sqrt(scale * total[0] / days)
    acc = total[1] / jnp.sqrt(total[2] * total[3] + 1e-06)
    rmse_ref[0] = rmse.reshape(VARS, TILE, DEST_MERIDIANS)
    acc_ref[0] = acc.reshape(VARS, TILE, DEST_MERIDIANS)


def maps(one, two, three, own):
    phi = (np.arange(DEST_PARALLELS, dtype=np.float32) + np.float32(0.5)) * np.float32(
        math.pi / DEST_PARALLELS
    ) - np.float32(0.5 * math.pi)
    cosine = np.cos(phi).astype(np.float32)
    scale = jnp.asarray(cosine / cosine.mean(dtype=np.float32))
    vmem = pl.BlockSpec(memory_space=pltpu.VMEM)
    shape = jax.ShapeDtypeStruct((1, VARS, TILE, DEST_MERIDIANS), jnp.float32)
    return pl.pallas_call(
        maps_kernel,
        in_specs=[pl.BlockSpec(memory_space=pltpu.SMEM)] + [vmem] * 4,
        out_specs=[vmem] * 2,
        out_shape=[shape] * 2,
        compiler_params=params(8),
        cost_estimate=cost(1),
        name="maps",
    )(scale, one, two, three, own)


def body(normals, index, extent, count, bins, prognosis, analysis):
    field = jnp.transpose(normals, (0, 2, 1, 3))
    own, cross_edge, inner_edge = lon_rows(field)
    devices, slots = lax.axis_size("lat"), lax.axis_size("slot")
    meets = [(i * slots + x, (i + 1) * slots + x) for i in range(1, devices - 1, 2) for x in range(slots)]
    ends = [(i * slots + x, i * slots + x + 1) for i in (0, devices - 1) for x in range(0, slots, 2)]
    meets = [pair for i, j in meets + ends for pair in ((i, j), (j, i))]
    cross = lax.ppermute(cross_edge, ("lat", "slot"), meets)
    inner = lax.ppermute(inner_edge, "lat", [(i, i ^ 1) for i in range(devices)])
    fore, obs, error, weights = relaid_days(index, extent, count, prognosis, analysis)
    low, high = climate_code(weights, cross, own, inner)
    left_low = shifted(low, 1)
    right_high = shifted(high, -1)
    left_high = shifted(high, 1)
    right_low = shifted(low, -1)
    far_low = shifted(left_low, 1)
    far_high = shifted(right_high, -1)
    near = decoded(low, high, right_low, right_high, left_low, left_high)
    wanted = jnp.transpose(bins)
    to_one, to_two, to_three, clim = other_sums(
        wanted, near, far_low, far_high, fore, obs, error
    )
    two = shifted(to_two, 2)
    one = shifted(to_one, 1)
    three = shifted(to_three, 3)
    mine = my_sums(wanted, clim, fore, obs, error)
    return tuple(maps(one, two, three, mine))


def solution(mesh):
    placed = (
        P("slot", None, "lat", None),
        P("lat", None),
        P("lat", None),
        P("lat"),
        P("slot", None),
        P("slot", None, None, "lat", None),
        P("slot", None, None, "lat", None),
    )

    return jax.shard_map(
        body,
        mesh=mesh,
        in_specs=placed,
        out_specs=(P("slot", None, "lat", None), P("slot", None, "lat", None)),
        check_vma=False,
    )
```

```python
import math

import jax
import jax.numpy as jnp
import numpy as np
from jax import lax
from jax.experimental import pallas as pl
from jax.experimental.pallas import tpu as pltpu
from jax.sharding import PartitionSpec as P

SRC_LON = 1440
DEST_PARALLELS = 128
DEST_MERIDIANS = 240
FINE = SRC_LON // DEST_MERIDIANS
VARS = 8
BAND = 22
TILE = 4
OVER = 10
EDGE = 3
MID = BAND - 2 * EDGE
ROWS = BAND + 2 * EDGE
SPAN = BAND + EDGE
BINS = 16
HALF = BINS // 2
DAYS = 32
SLOTS = 4
FLAT = VARS * TILE
EDGE_LIMIT = 57
MID_LIMIT = 50
CODE_RATE = 10.0
CODE_BASE = 120.0
SUM_SCALE = 64.0
SUM_FLOOR = 2.0**-126


def shifted(value, step):
    slots = lax.axis_size("slot")
    return lax.ppermute(value, "slot", [(i, (i + step) % slots) for i in range(slots)])


def fill_table(table_ref):
    lines = 96
    line = lax.broadcasted_iota(jnp.int32, (lines, DEST_MERIDIANS), 0)
    start = FINE * lax.broadcasted_iota(jnp.int32, (lines, DEST_MERIDIANS), 1)
    for first in range(0, SRC_LON, lines):
        place = line + first - start
        inside = (place >= 0) & (place < FINE)
        table_ref[first : first + lines] = jnp.where(inside, 1.0, 0.0).astype(jnp.bfloat16)


def lon_mean(rows, table):
    flat = rows.reshape(-1, SRC_LON)
    total = jnp.dot(flat, table, preferred_element_type=jnp.float32)
    return (total * (1.0 / FINE)).astype(jnp.bfloat16).reshape(*rows.shape[:-1], DEST_MERIDIANS)


def params(mebibytes):
    return pltpu.CompilerParams(vmem_limit_bytes=mebibytes * 1024 * 1024)


def cost(microseconds):
    return pl.CostEstimate(
        flops=0, bytes_accessed=int(microseconds * 3 * 10**6), transcendentals=0
    )


def edge_kernel(field_ref, cross_ref, inner_ref, buf, table_buf, sems):
    odd = lax.rem(lax.axis_index("lat"), 2)
    firsts = (odd * (BAND - EDGE), (1 - odd) * (BAND - EDGE))
    outs = (cross_ref, inner_ref)
    jobs = []
    for n, first in enumerate(firsts):
        for part in range(2):
            some = pl.ds(part * HALF, HALF)
            copy = pltpu.make_async_copy(
                field_ref.at[some, pl.ds(first, EDGE)], buf.at[n, some], sems.at[2 * n + part]
            )
            copy.start()
            jobs.append((copy, n, slice(part * HALF, (part + 1) * HALF)))
    fill_table(table_buf)
    for copy, n, some in jobs:
        copy.wait()
        for s in range(some.start, some.stop, 4):
            outs[n][s : s + 4] = lon_mean(buf[n, s : s + 4], table_buf[...])


def edge_rows(field):
    vmem = pl.BlockSpec(memory_space=pltpu.VMEM)
    return pl.pallas_call(
        edge_kernel,
        in_specs=[pl.BlockSpec(memory_space=pl.ANY)],
        out_specs=[vmem] * 2,
        out_shape=[jax.ShapeDtypeStruct((BINS, EDGE, VARS, DEST_MERIDIANS), jnp.bfloat16)] * 2,
        scratch_shapes=[
            pltpu.VMEM((2, BINS, EDGE, VARS, SRC_LON), jnp.bfloat16),
            pltpu.VMEM((SRC_LON, DEST_MERIDIANS), jnp.bfloat16),
            pltpu.SemaphoreType.DMA((4,)),
        ],
        compiler_params=params(EDGE_LIMIT),
        cost_estimate=cost(2),
        name="edge_rows",
    )(field)


def mid_kernel(
    field_ref, index_ref, extent_ref, count_ref, out_ref, weights_ref,
    buf, table_buf, index_buf, extent_buf, count_buf, sems, small_sems,
):
    parts = sems.shape[0]
    size = BINS // parts
    block = 2
    lists = ((index_ref, index_buf), (extent_ref, extent_buf), (count_ref, count_buf))
    loads = [pltpu.make_async_copy(a, b, small_sems.at[n]) for n, (a, b) in enumerate(lists)]
    copies = []
    for n in range(parts):
        some = pl.ds(n * size, size)
        copies.append(
            pltpu.make_async_copy(field_ref.at[some, pl.ds(EDGE, MID)], buf.at[some], sems.at[n])
        )
    for copy in loads + copies:
        copy.start()
    fill_table(table_buf)
    for copy in loads:
        copy.wait()
    weights_ref[...] = weight_matrix(index_buf, extent_buf, count_buf)
    for first in range(0, BINS, block):
        if first % size == 0:
            copies[first // size].wait()
        some = slice(first, first + block)
        out_ref[some] = lon_mean(buf[some], table_buf[...])


def mid_rows(field, index, extent, count):
    parts = 4
    hbm = pl.BlockSpec(memory_space=pl.ANY)
    vmem = pl.BlockSpec(memory_space=pltpu.VMEM)
    return pl.pallas_call(
        mid_kernel,
        in_specs=[hbm] * 4,
        out_specs=[vmem] * 2,
        out_shape=[
            jax.ShapeDtypeStruct((BINS, MID, VARS, DEST_MERIDIANS), jnp.bfloat16),
            jax.ShapeDtypeStruct((3 * FLAT, ROWS * VARS), jnp.bfloat16),
        ],
        scratch_shapes=[
            pltpu.VMEM((BINS, MID, VARS, SRC_LON), jnp.bfloat16),
            pltpu.VMEM((SRC_LON, DEST_MERIDIANS), jnp.bfloat16),
            pltpu.SMEM((TILE, OVER), jnp.int32),
            pltpu.SMEM((TILE, OVER), jnp.float32),
            pltpu.SMEM((TILE,), jnp.int32),
            pltpu.SemaphoreType.DMA((parts,)),
            pltpu.SemaphoreType.DMA((3,)),
        ],
        compiler_params=params(MID_LIMIT),
        cost_estimate=cost(4),
        name="mid_rows",
    )(field, index, extent, count)


def encode(value):
    size = jnp.exp2(CODE_RATE * jnp.abs(value) - CODE_BASE)
    return jnp.where(value < 0, -size, size).astype(jnp.bfloat16)


def decode(code):
    wide = code.astype(jnp.float32)
    size = (jnp.log2(jnp.abs(wide)) + CODE_BASE) * (1.0 / CODE_RATE)
    return jnp.where(wide < 0, -size, size)


def weight_matrix(index_ref, extent_ref, count_ref):
    lat = lax.axis_index("lat")
    odd = lax.rem(lat, 2) == 1
    line = lax.broadcasted_iota(jnp.int32, (FLAT, ROWS * VARS), 0)
    lane = lax.broadcasted_iota(jnp.int32, (FLAT, ROWS * VARS), 1)
    place = jnp.where(line // TILE == lane % VARS, lane // VARS, -1)
    dense = jnp.zeros((FLAT, ROWS * VARS), jnp.float32)
    sums = jnp.ones((FLAT, ROWS * VARS), jnp.float32)
    for t in range(TILE):
        here = line % TILE == t
        spot = jnp.where(here, place, -1)
        total = jnp.float32(0.0)
        for k in range(OVER):
            value = jnp.where(k < count_ref[t], extent_ref[t, k], jnp.float32(0.0))
            total = total + value
            row = index_ref[t, k] - lat * BAND
            inside = (row >= EDGE) & (row < BAND - EDGE)
            shift = jnp.where(inside, 0, jnp.where(row < 0, SPAN, -SPAN))
            shift = jnp.where((row >= 0) & (row < EDGE), BAND - EDGE, shift)
            shift = jnp.where((row >= BAND - EDGE) & (row < BAND), EDGE - BAND, shift)
            column = row + EDGE + jnp.where(odd, shift, 0)
            dense = dense + jnp.where(spot == column, value, 0.0)
        sums = jnp.where(here, total, sums)
    dense = dense / sums
    high = dense.astype(jnp.bfloat16)
    rest = dense - high.astype(jnp.float32)
    middle_part = rest.astype(jnp.bfloat16)
    low = (rest - middle_part.astype(jnp.float32)).astype(jnp.bfloat16)
    return jnp.concatenate([high, middle_part, low], axis=0)


def climate_kernel(
    weights_ref, cross_ref, cross_own, mid_ref, inner_own, inner_ref, low_ref, high_ref
):
    weights = weights_ref[...]
    refs = (cross_ref, cross_own, mid_ref, inner_own, inner_ref)
    for s in range(BINS):
        rows = jnp.concatenate([ref[s] for ref in refs], axis=0)
        rows = rows.reshape(ROWS * VARS, DEST_MERIDIANS)
        parts = jnp.dot(weights, rows, preferred_element_type=jnp.float32)
        value = parts[:FLAT] + parts[FLAT : 2 * FLAT] + parts[2 * FLAT :]
        out_ref = low_ref if s < HALF else high_ref
        out_ref[s % HALF] = encode(value)


def climate_code(*arrays):
    vmem = pl.BlockSpec(memory_space=pltpu.VMEM)
    return pl.pallas_call(
        climate_kernel,
        in_specs=[vmem] * 6,
        out_specs=[vmem] * 2,
        out_shape=[jax.ShapeDtypeStruct((HALF, FLAT, DEST_MERIDIANS), jnp.bfloat16)] * 2,
        compiler_params=params(8),
        cost_estimate=cost(1),
        name="climate",
    )(*arrays)


def days_kernel(fore_ref, obs_ref, fore_out, obs_out, error_out):
    slot = lax.axis_index("slot")
    for k in range(SLOTS):
        lead = lax.rem(slot + k, SLOTS)

        def step(d, squared):
            fore = fore_ref[d, lead].astype(jnp.float32).reshape(FLAT, DEST_MERIDIANS)
            obs = obs_ref[d, lead].astype(jnp.float32).reshape(FLAT, DEST_MERIDIANS)
            fore_out[k, d] = fore
            obs_out[k, d] = obs
            error = fore - obs
            return squared + error * error

        zero = jnp.zeros((FLAT, DEST_MERIDIANS), jnp.float32)
        error_out[k] = lax.fori_loop(0, DAYS, step, zero, unroll=2)


def relaid_days(fore, obs):
    vmem = pl.BlockSpec(memory_space=pltpu.VMEM)
    grid = jax.ShapeDtypeStruct((SLOTS, DAYS, FLAT, DEST_MERIDIANS), jnp.float32)
    return pl.pallas_call(
        days_kernel,
        in_specs=[vmem] * 2,
        out_specs=[vmem] * 3,
        out_shape=[grid, grid, jax.ShapeDtypeStruct((SLOTS, FLAT, DEST_MERIDIANS), jnp.float32)],
        compiler_params=params(20),
        cost_estimate=cost(2),
        name="days",
    )(fore, obs)


def decode_kernel(*refs):
    near_ref = refs[-1]
    for n, code_ref in enumerate(refs[:-1]):
        near_ref[n * HALF : (n + 1) * HALF] = decode(code_ref[...])


def decoded(*codes):
    vmem = pl.BlockSpec(memory_space=pltpu.VMEM)
    return pl.pallas_call(
        decode_kernel,
        in_specs=[vmem] * len(codes),
        out_specs=vmem,
        out_shape=jax.ShapeDtypeStruct((len(codes) * HALF, FLAT, DEST_MERIDIANS), jnp.float32),
        compiler_params=params(8),
        cost_estimate=cost(1),
        name="decode",
    )(*codes)


def encode_sum(value):
    scaled = value * SUM_SCALE
    square = scaled * scaled
    power = square * square * square
    return jnp.where(value < 0, -power, power).astype(jnp.bfloat16)


def decode_sum(code):
    wide = code.astype(jnp.float32)
    size = jnp.maximum(jnp.abs(wide), SUM_FLOOR)
    root = jnp.exp2(jnp.log2(size) * (1.0 / 6.0)) * (1.0 / SUM_SCALE)
    return jnp.where(wide < 0, -root, root)


def lead_sums(k, bins_ref, clim_ref, fore_ref, obs_ref, error_ref, out_ref, kept):
    slot = lax.axis_index("slot")
    lead = lax.rem(slot + k, SLOTS)
    first = slot * BINS
    half = FLAT // 2
    for h in range(2):
        some = slice(h * half, (h + 1) * half)

        def step(d, sums):
            cross, fore_sq, true_sq = sums
            clim = clim_ref[(bins_ref[lead, d] - first) & (SLOTS * BINS - 1), some]
            fore_anom = fore_ref[k, d, some] - clim
            true_anom = obs_ref[k, d, some] - clim
            return (
                cross + fore_anom * true_anom,
                fore_sq + fore_anom * fore_anom,
                true_sq + true_anom * true_anom,
            )

        zero = jnp.zeros((half, DEST_MERIDIANS), jnp.float32)
        sums = lax.fori_loop(0, DAYS, step, (zero,) * 3, unroll=8)
        for n, value in enumerate(sums):
            out_ref[n + 1, some] = kept(value)
    out_ref[0] = kept(error_ref[k])


def others_kernel(
    bins_ref, near_ref, low_ref, high_ref, fore_ref, obs_ref, error_ref,
    one_ref, two_ref, three_ref, clim_ref,
):
    clim_ref[: 2 * BINS] = near_ref[: 2 * BINS]
    clim_ref[3 * BINS :] = near_ref[2 * BINS :]
    clim_ref[2 * BINS : 2 * BINS + HALF] = decode(low_ref[...])
    clim_ref[2 * BINS + HALF : 3 * BINS] = decode(high_ref[...])
    for k, out_ref in ((1, one_ref), (2, two_ref), (3, three_ref)):
        lead_sums(k, bins_ref, clim_ref, fore_ref, obs_ref, error_ref, out_ref, encode_sum)


def mine_kernel(bins_ref, clim_ref, fore_ref, obs_ref, error_ref, out_ref):
    lead_sums(0, bins_ref, clim_ref, fore_ref, obs_ref, error_ref, out_ref, lambda value: value)


def other_sums(bins, near, low, high, fore, obs, error):
    vmem = pl.BlockSpec(memory_space=pltpu.VMEM)
    code = jax.ShapeDtypeStruct((4, FLAT, DEST_MERIDIANS), jnp.bfloat16)
    whole = jax.ShapeDtypeStruct((SLOTS * BINS, FLAT, DEST_MERIDIANS), jnp.float32)
    return pl.pallas_call(
        others_kernel,
        in_specs=[pl.BlockSpec(memory_space=pltpu.SMEM)] + [vmem] * 6,
        out_specs=[vmem] * 4,
        out_shape=[code, code, code, whole],
        compiler_params=params(16),
        cost_estimate=cost(3),
        name="other_sums",
    )(bins, near, low, high, fore, obs, error)


def my_sums(bins, clim, fore, obs, error):
    vmem = pl.BlockSpec(memory_space=pltpu.VMEM)
    return pl.pallas_call(
        mine_kernel,
        in_specs=[pl.BlockSpec(memory_space=pltpu.SMEM)] + [vmem] * 4,
        out_specs=vmem,
        out_shape=jax.ShapeDtypeStruct((4, FLAT, DEST_MERIDIANS), jnp.float32),
        compiler_params=params(16),
        cost_estimate=cost(1),
        name="my_sums",
    )(bins, clim, fore, obs, error)


def maps_kernel(scale_ref, one_ref, two_ref, three_ref, own_ref, rmse_ref, acc_ref):
    lat = lax.axis_index("lat")
    total = own_ref[...]
    for code_ref in (one_ref, two_ref, three_ref):
        total = total + decode_sum(code_ref[...])
    line = lax.broadcasted_iota(jnp.int32, (FLAT, DEST_MERIDIANS), 0)
    scale = jnp.zeros((FLAT, DEST_MERIDIANS), jnp.float32)
    for t in range(TILE):
        scale = jnp.where(line % TILE == t, scale_ref[lat * TILE + t], scale)
    days = DAYS * SLOTS
    rmse = jnp.sqrt(scale * total[0] / days)
    acc = total[1] / jnp.sqrt(total[2] * total[3] + 1e-06)
    rmse_ref[0] = rmse.reshape(VARS, TILE, DEST_MERIDIANS)
    acc_ref[0] = acc.reshape(VARS, TILE, DEST_MERIDIANS)


def maps(one, two, three, own):
    phi = (np.arange(DEST_PARALLELS, dtype=np.float32) + np.float32(0.5)) * np.float32(
        math.pi / DEST_PARALLELS
    ) - np.float32(0.5 * math.pi)
    cosine = np.cos(phi).astype(np.float32)
    scale = jnp.asarray(cosine / cosine.mean(dtype=np.float32))
    vmem = pl.BlockSpec(memory_space=pltpu.VMEM)
    shape = jax.ShapeDtypeStruct((1, VARS, TILE, DEST_MERIDIANS), jnp.float32)
    return pl.pallas_call(
        maps_kernel,
        in_specs=[pl.BlockSpec(memory_space=pltpu.SMEM)] + [vmem] * 4,
        out_specs=[vmem] * 2,
        out_shape=[shape] * 2,
        compiler_params=params(8),
        cost_estimate=cost(1),
        name="maps",
    )(scale, one, two, three, own)


def body(normals, index, extent, count, bins, prognosis, analysis):
    field = jnp.transpose(normals, (0, 2, 1, 3))
    cross_own, inner_own = edge_rows(field)
    devices, slots = lax.axis_size("lat"), lax.axis_size("slot")
    meets = [(i * slots + x, (i + 1) * slots + x) for i in range(1, devices - 1, 2) for x in range(slots)]
    meets += [(i * slots + x, i * slots + x + 1) for i in (0, devices - 1) for x in range(0, slots, 2)]
    meets = [pair for i, j in meets for pair in ((i, j), (j, i))]
    cross = lax.ppermute(cross_own, ("lat", "slot"), meets)
    inner = lax.ppermute(inner_own, "lat", [(i, i ^ 1) for i in range(devices)])
    mid, weights = mid_rows(field, index, extent, count)
    low, high = climate_code(weights, cross, cross_own, mid, inner_own, inner)
    left_low = shifted(low, 1)
    right_high = shifted(high, -1)
    left_high = shifted(high, 1)
    right_low = shifted(low, -1)
    far_low = shifted(left_low, 1)
    far_high = shifted(right_high, -1)
    fore, obs, error = relaid_days(prognosis, analysis)
    near = decoded(low, high, right_low, right_high, left_low, left_high)
    wanted = jnp.transpose(bins)
    to_one, to_two, to_three, clim = other_sums(
        wanted, near, far_low, far_high, fore, obs, error
    )
    two = shifted(to_two, 2)
    one = shifted(to_one, 1)
    three = shifted(to_three, 3)
    mine = my_sums(wanted, clim, fore, obs, error)
    return tuple(maps(one, two, three, mine))


def solution(mesh):
    placed = (
        P("slot", None, "lat", None),
        P("lat", None),
        P("lat", None),
        P("lat"),
        P("slot", None),
        P("slot", None, None, "lat", None),
        P("slot", None, None, "lat", None),
    )

    return jax.shard_map(
        body,
        mesh=mesh,
        in_specs=placed,
        out_specs=(P("slot", None, "lat", None), P("slot", None, "lat", None)),
        check_vma=False,
    )
```

```python
import math

import jax
import jax.numpy as jnp
import numpy as np
from jax import lax
from jax.experimental import pallas as pl
from jax.experimental.pallas import tpu as pltpu
from jax.sharding import PartitionSpec as P

SRC_LON = 1440
DEST_PARALLELS = 128
DEST_MERIDIANS = 240
FINE = SRC_LON // DEST_MERIDIANS
VARS = 8
BAND = 22
TILE = 4
OVER = 10
EDGE = 3
MID = BAND - 2 * EDGE
ROWS = BAND + 2 * EDGE
SPAN = BAND + EDGE
BINS = 16
HALF = BINS // 2
DAYS = 32
SLOTS = 4
FLAT = VARS * TILE
EDGE_LIMIT = 52
MID_LIMIT = 50
CODE_RATE = 10.0
CODE_BASE = 120.0
SUM_SCALE = 64.0
SUM_FLOOR = 2.0**-126


def shifted(value, step):
    slots = lax.axis_size("slot")
    return lax.ppermute(value, "slot", [(i, (i + step) % slots) for i in range(slots)])


def fill_table(table_ref):
    lines = 96
    line = lax.broadcasted_iota(jnp.int32, (lines, DEST_MERIDIANS), 0)
    start = FINE * lax.broadcasted_iota(jnp.int32, (lines, DEST_MERIDIANS), 1)
    for first in range(0, SRC_LON, lines):
        place = line + first - start
        inside = (place >= 0) & (place < FINE)
        table_ref[first : first + lines] = jnp.where(inside, 1.0, 0.0).astype(jnp.bfloat16)


def lon_mean(rows, table):
    flat = rows.reshape(-1, SRC_LON)
    total = jnp.dot(flat, table, preferred_element_type=jnp.float32)
    return (total * (1.0 / FINE)).astype(jnp.bfloat16).reshape(*rows.shape[:-1], DEST_MERIDIANS)


def params(mebibytes):
    return pltpu.CompilerParams(vmem_limit_bytes=mebibytes * 1024 * 1024)


def cost(microseconds):
    return pl.CostEstimate(
        flops=0, bytes_accessed=int(microseconds * 3 * 10**6), transcendentals=0
    )


def edge_kernel(field_ref, cross_ref, inner_ref, buf, table_buf, sems):
    odd = lax.rem(lax.axis_index("lat"), 2)
    firsts = (odd * (BAND - EDGE), (1 - odd) * (BAND - EDGE))
    outs = (cross_ref, inner_ref)
    jobs = []
    for n, first in enumerate(firsts):
        for part in range(2):
            some = pl.ds(part * HALF, HALF)
            copy = pltpu.make_async_copy(
                field_ref.at[some, pl.ds(first, EDGE)], buf.at[n, some], sems.at[2 * n + part]
            )
            copy.start()
            jobs.append((copy, n, slice(part * HALF, (part + 1) * HALF)))
    fill_table(table_buf)
    for copy, n, some in jobs:
        copy.wait()
        for s in range(some.start, some.stop, 4):
            outs[n][s : s + 4] = lon_mean(buf[n, s : s + 4], table_buf[...])


def edge_rows(field):
    vmem = pl.BlockSpec(memory_space=pltpu.VMEM)
    return pl.pallas_call(
        edge_kernel,
        in_specs=[pl.BlockSpec(memory_space=pl.ANY)],
        out_specs=[vmem] * 2,
        out_shape=[jax.ShapeDtypeStruct((BINS, EDGE, VARS, DEST_MERIDIANS), jnp.bfloat16)] * 2,
        scratch_shapes=[
            pltpu.VMEM((2, BINS, EDGE, VARS, SRC_LON), jnp.bfloat16),
            pltpu.VMEM((SRC_LON, DEST_MERIDIANS), jnp.bfloat16),
            pltpu.SemaphoreType.DMA((4,)),
        ],
        compiler_params=params(EDGE_LIMIT),
        cost_estimate=cost(2),
        name="edge_rows",
    )(field)


def mid_kernel(
    field_ref, index_ref, extent_ref, count_ref, out_ref, weights_ref,
    buf, table_buf, index_buf, extent_buf, count_buf, sems, small_sems,
):
    parts = sems.shape[0]
    size = BINS // parts
    block = 2
    lists = ((index_ref, index_buf), (extent_ref, extent_buf), (count_ref, count_buf))
    loads = [pltpu.make_async_copy(a, b, small_sems.at[n]) for n, (a, b) in enumerate(lists)]
    copies = []
    for n in range(parts):
        some = pl.ds(n * size, size)
        copies.append(
            pltpu.make_async_copy(field_ref.at[some, pl.ds(EDGE, MID)], buf.at[some], sems.at[n])
        )
    for copy in loads + copies:
        copy.start()
    fill_table(table_buf)
    for copy in loads:
        copy.wait()
    weights_ref[...] = weight_matrix(index_buf, extent_buf, count_buf)
    for first in range(0, BINS, block):
        if first % size == 0:
            copies[first // size].wait()
        some = slice(first, first + block)
        out_ref[some] = lon_mean(buf[some], table_buf[...])


def mid_rows(field, index, extent, count):
    parts = 4
    hbm = pl.BlockSpec(memory_space=pl.ANY)
    vmem = pl.BlockSpec(memory_space=pltpu.VMEM)
    return pl.pallas_call(
        mid_kernel,
        in_specs=[hbm] * 4,
        out_specs=[vmem] * 2,
        out_shape=[
            jax.ShapeDtypeStruct((BINS, MID, VARS, DEST_MERIDIANS), jnp.bfloat16),
            jax.ShapeDtypeStruct((3 * FLAT, ROWS * VARS), jnp.bfloat16),
        ],
        scratch_shapes=[
            pltpu.VMEM((BINS, MID, VARS, SRC_LON), jnp.bfloat16),
            pltpu.VMEM((SRC_LON, DEST_MERIDIANS), jnp.bfloat16),
            pltpu.SMEM((TILE, OVER), jnp.int32),
            pltpu.SMEM((TILE, OVER), jnp.float32),
            pltpu.SMEM((TILE,), jnp.int32),
            pltpu.SemaphoreType.DMA((parts,)),
            pltpu.SemaphoreType.DMA((3,)),
        ],
        compiler_params=params(MID_LIMIT),
        cost_estimate=cost(4),
        name="mid_rows",
    )(field, index, extent, count)


def encode(value):
    size = jnp.exp2(CODE_RATE * jnp.abs(value) - CODE_BASE)
    return jnp.where(value < 0, -size, size).astype(jnp.bfloat16)


def decode(code):
    wide = code.astype(jnp.float32)
    size = (jnp.log2(jnp.abs(wide)) + CODE_BASE) * (1.0 / CODE_RATE)
    size = jnp.where(jnp.abs(wide) > 2.0**-CODE_BASE, size, 0.0)
    return jnp.where(wide < 0, -size, size)


def weight_matrix(index_ref, extent_ref, count_ref):
    lat = lax.axis_index("lat")
    odd = lax.rem(lat, 2) == 1
    line = lax.broadcasted_iota(jnp.int32, (FLAT, ROWS * VARS), 0)
    lane = lax.broadcasted_iota(jnp.int32, (FLAT, ROWS * VARS), 1)
    place = jnp.where(line // TILE == lane % VARS, lane // VARS, -1)
    dense = jnp.zeros((FLAT, ROWS * VARS), jnp.float32)
    sums = jnp.ones((FLAT, ROWS * VARS), jnp.float32)
    for t in range(TILE):
        here = line % TILE == t
        spot = jnp.where(here, place, -1)
        total = jnp.float32(0.0)
        for k in range(OVER):
            value = jnp.where(k < count_ref[t], extent_ref[t, k], jnp.float32(0.0))
            total = total + value
            row = index_ref[t, k] - lat * BAND
            inside = (row >= EDGE) & (row < BAND - EDGE)
            shift = jnp.where(inside, 0, jnp.where(row < 0, SPAN, -SPAN))
            shift = jnp.where((row >= 0) & (row < EDGE), BAND - EDGE, shift)
            shift = jnp.where((row >= BAND - EDGE) & (row < BAND), EDGE - BAND, shift)
            column = row + EDGE + jnp.where(odd, shift, 0)
            dense = dense + jnp.where(spot == column, value, 0.0)
        sums = jnp.where(here, total, sums)
    dense = dense / sums
    high = dense.astype(jnp.bfloat16)
    rest = dense - high.astype(jnp.float32)
    middle_part = rest.astype(jnp.bfloat16)
    low = (rest - middle_part.astype(jnp.float32)).astype(jnp.bfloat16)
    return jnp.concatenate([high, middle_part, low], axis=0)


def climate_kernel(
    weights_ref, cross_ref, cross_own, mid_ref, inner_own, inner_ref, low_ref, high_ref
):
    weights = weights_ref[...]
    refs = (cross_ref, cross_own, mid_ref, inner_own, inner_ref)
    for s in range(BINS):
        rows = jnp.concatenate([ref[s] for ref in refs], axis=0)
        rows = rows.reshape(ROWS * VARS, DEST_MERIDIANS)
        parts = jnp.dot(weights, rows, preferred_element_type=jnp.float32)
        value = parts[:FLAT] + parts[FLAT : 2 * FLAT] + parts[2 * FLAT :]
        out_ref = low_ref if s < HALF else high_ref
        out_ref[s % HALF] = encode(value)


def climate_code(*arrays):
    vmem = pl.BlockSpec(memory_space=pltpu.VMEM)
    return pl.pallas_call(
        climate_kernel,
        in_specs=[vmem] * 6,
        out_specs=[vmem] * 2,
        out_shape=[jax.ShapeDtypeStruct((HALF, FLAT, DEST_MERIDIANS), jnp.bfloat16)] * 2,
        compiler_params=params(8),
        cost_estimate=cost(1),
        name="climate",
    )(*arrays)


def days_kernel(fore_ref, obs_ref, fore_out, obs_out, error_out):
    slot = lax.axis_index("slot")
    for k in range(SLOTS):
        lead = lax.rem(slot + k, SLOTS)

        def step(d, squared):
            fore = fore_ref[d, lead].astype(jnp.float32).reshape(FLAT, DEST_MERIDIANS)
            obs = obs_ref[d, lead].astype(jnp.float32).reshape(FLAT, DEST_MERIDIANS)
            fore_out[k, d] = fore
            obs_out[k, d] = obs
            error = fore - obs
            return squared + error * error

        zero = jnp.zeros((FLAT, DEST_MERIDIANS), jnp.float32)
        error_out[k] = lax.fori_loop(0, DAYS, step, zero, unroll=2)


def relaid_days(fore, obs):
    vmem = pl.BlockSpec(memory_space=pltpu.VMEM)
    grid = jax.ShapeDtypeStruct((SLOTS, DAYS, FLAT, DEST_MERIDIANS), jnp.float32)
    return pl.pallas_call(
        days_kernel,
        in_specs=[vmem] * 2,
        out_specs=[vmem] * 3,
        out_shape=[grid, grid, jax.ShapeDtypeStruct((SLOTS, FLAT, DEST_MERIDIANS), jnp.float32)],
        compiler_params=params(20),
        cost_estimate=cost(2),
        name="days",
    )(fore, obs)


def decode_kernel(*refs):
    near_ref = refs[-1]
    for n, code_ref in enumerate(refs[:-1]):
        near_ref[n * HALF : (n + 1) * HALF] = decode(code_ref[...])


def decoded(*codes):
    vmem = pl.BlockSpec(memory_space=pltpu.VMEM)
    return pl.pallas_call(
        decode_kernel,
        in_specs=[vmem] * len(codes),
        out_specs=vmem,
        out_shape=jax.ShapeDtypeStruct((len(codes) * HALF, FLAT, DEST_MERIDIANS), jnp.float32),
        compiler_params=params(8),
        cost_estimate=cost(1),
        name="decode",
    )(*codes)


def encode_sum(value):
    scaled = value * SUM_SCALE
    square = scaled * scaled
    power = square * square * square
    return jnp.where(value < 0, -power, power).astype(jnp.bfloat16)


def decode_sum(code):
    wide = code.astype(jnp.float32)
    size = jnp.maximum(jnp.abs(wide), SUM_FLOOR)
    root = jnp.exp2(jnp.log2(size) * (1.0 / 6.0)) * (1.0 / SUM_SCALE)
    root = jnp.where(wide == 0, 0.0, root)
    return jnp.where(wide < 0, -root, root)


def lead_sums(k, bins_ref, clim_ref, fore_ref, obs_ref, error_ref, out_ref, kept):
    slot = lax.axis_index("slot")
    lead = lax.rem(slot + k, SLOTS)
    first = slot * BINS
    half = FLAT // 2
    for h in range(2):
        some = slice(h * half, (h + 1) * half)

        def step(d, sums):
            cross, fore_sq, true_sq = sums
            clim = clim_ref[(bins_ref[lead, d] - first) & (SLOTS * BINS - 1), some]
            fore_anom = fore_ref[k, d, some] - clim
            true_anom = obs_ref[k, d, some] - clim
            return (
                cross + fore_anom * true_anom,
                fore_sq + fore_anom * fore_anom,
                true_sq + true_anom * true_anom,
            )

        zero = jnp.zeros((half, DEST_MERIDIANS), jnp.float32)
        sums = lax.fori_loop(0, DAYS, step, (zero,) * 3, unroll=16)
        for n, value in enumerate(sums):
            out_ref[n + 1, some] = kept(value)
    out_ref[0] = kept(error_ref[k])


def others_kernel(
    bins_ref, near_ref, low_ref, high_ref, fore_ref, obs_ref, error_ref,
    one_ref, two_ref, three_ref, clim_ref,
):
    clim_ref[: 2 * BINS] = near_ref[: 2 * BINS]
    clim_ref[3 * BINS :] = near_ref[2 * BINS :]
    clim_ref[2 * BINS : 2 * BINS + HALF] = decode(low_ref[...])
    clim_ref[2 * BINS + HALF : 3 * BINS] = decode(high_ref[...])
    for k, out_ref in ((1, one_ref), (2, two_ref), (3, three_ref)):
        lead_sums(k, bins_ref, clim_ref, fore_ref, obs_ref, error_ref, out_ref, encode_sum)


def mine_kernel(
    bins_ref, scale_ref, clim_ref, fore_ref, obs_ref, error_ref, out_ref, scale_out
):
    lat = lax.axis_index("lat")
    line = lax.broadcasted_iota(jnp.int32, (FLAT, DEST_MERIDIANS), 0)
    scale = jnp.zeros((FLAT, DEST_MERIDIANS), jnp.float32)
    for t in range(TILE):
        scale = jnp.where(line % TILE == t, scale_ref[lat * TILE + t], scale)
    scale_out[...] = scale
    lead_sums(0, bins_ref, clim_ref, fore_ref, obs_ref, error_ref, out_ref, lambda value: value)


def other_sums(bins, near, low, high, fore, obs, error):
    vmem = pl.BlockSpec(memory_space=pltpu.VMEM)
    code = jax.ShapeDtypeStruct((4, FLAT, DEST_MERIDIANS), jnp.bfloat16)
    whole = jax.ShapeDtypeStruct((SLOTS * BINS, FLAT, DEST_MERIDIANS), jnp.float32)
    return pl.pallas_call(
        others_kernel,
        in_specs=[pl.BlockSpec(memory_space=pltpu.SMEM)] + [vmem] * 6,
        out_specs=[vmem] * 4,
        out_shape=[code, code, code, whole],
        compiler_params=params(16),
        cost_estimate=cost(3),
        name="other_sums",
    )(bins, near, low, high, fore, obs, error)


def lat_weights():
    phi = (np.arange(DEST_PARALLELS, dtype=np.float32) + np.float32(0.5)) * np.float32(
        math.pi / DEST_PARALLELS
    ) - np.float32(0.5 * math.pi)
    cosine = np.cos(phi).astype(np.float32)
    return jnp.asarray(cosine / cosine.mean(dtype=np.float32))


def my_sums(bins, clim, fore, obs, error):
    smem = pl.BlockSpec(memory_space=pltpu.SMEM)
    vmem = pl.BlockSpec(memory_space=pltpu.VMEM)
    return pl.pallas_call(
        mine_kernel,
        in_specs=[smem] * 2 + [vmem] * 4,
        out_specs=[vmem] * 2,
        out_shape=[
            jax.ShapeDtypeStruct((4, FLAT, DEST_MERIDIANS), jnp.float32),
            jax.ShapeDtypeStruct((FLAT, DEST_MERIDIANS), jnp.float32),
        ],
        compiler_params=params(20),
        cost_estimate=cost(1),
        name="my_sums",
    )(bins, lat_weights(), clim, fore, obs, error)


def maps_kernel(one_ref, two_ref, three_ref, own_ref, scale_ref, rmse_ref, acc_ref):
    total = own_ref[...]
    for code_ref in (one_ref, two_ref, three_ref):
        total = total + decode_sum(code_ref[...])
    rmse = jnp.sqrt(scale_ref[...] * total[0] / (DAYS * SLOTS))
    acc = total[1] / jnp.sqrt(total[2] * total[3] + 1e-06)
    rmse_ref[0] = rmse.reshape(VARS, TILE, DEST_MERIDIANS)
    acc_ref[0] = acc.reshape(VARS, TILE, DEST_MERIDIANS)


def maps(*arrays):
    vmem = pl.BlockSpec(memory_space=pltpu.VMEM)
    shape = jax.ShapeDtypeStruct((1, VARS, TILE, DEST_MERIDIANS), jnp.float32)
    return pl.pallas_call(
        maps_kernel,
        in_specs=[vmem] * 5,
        out_specs=[vmem] * 2,
        out_shape=[shape] * 2,
        compiler_params=params(8),
        cost_estimate=cost(1),
        name="maps",
    )(*arrays)


def body(normals, index, extent, count, bins, prognosis, analysis):
    field = jnp.transpose(normals, (0, 2, 1, 3))
    cross_own, inner_own = edge_rows(field)
    devices, slots = lax.axis_size("lat"), lax.axis_size("slot")
    meets = [(i * slots + x, (i + 1) * slots + x) for i in range(1, devices - 1, 2) for x in range(slots)]
    meets += [(i * slots + x, i * slots + x + 1) for i in (0, devices - 1) for x in range(0, slots, 2)]
    meets = [pair for i, j in meets for pair in ((i, j), (j, i))]
    cross = lax.ppermute(cross_own, ("lat", "slot"), meets)
    inner = lax.ppermute(inner_own, "lat", [(i, i ^ 1) for i in range(devices)])
    mid, weights = mid_rows(field, index, extent, count)
    low, high = climate_code(weights, cross, cross_own, mid, inner_own, inner)
    left_low = shifted(low, 1)
    right_high = shifted(high, -1)
    left_high = shifted(high, 1)
    right_low = shifted(low, -1)
    far_low = shifted(left_low, 1)
    far_high = shifted(right_high, -1)
    fore, obs, error = relaid_days(prognosis, analysis)
    near = decoded(low, high, right_low, right_high, left_low, left_high)
    wanted = jnp.transpose(bins)
    to_one, to_two, to_three, clim = other_sums(
        wanted, near, far_low, far_high, fore, obs, error
    )
    two = shifted(to_two, 2)
    one = shifted(to_one, 1)
    three = shifted(to_three, 3)
    mine, scale = my_sums(wanted, clim, fore, obs, error)
    return tuple(maps(one, two, three, mine, scale))


def solution(mesh):
    placed = (
        P("slot", None, "lat", None),
        P("lat", None),
        P("lat", None),
        P("lat"),
        P("slot", None),
        P("slot", None, None, "lat", None),
        P("slot", None, None, "lat", None),
    )

    return jax.shard_map(
        body,
        mesh=mesh,
        in_specs=placed,
        out_specs=(P("slot", None, "lat", None), P("slot", None, "lat", None)),
        check_vma=False,
    )
```

```python
import math

import jax
import jax.numpy as jnp
import numpy as np
from jax import lax
from jax.experimental import pallas as pl
from jax.experimental.pallas import tpu as pltpu
from jax.sharding import PartitionSpec as P

SRC_LON = 1440
DEST_PARALLELS = 128
DEST_MERIDIANS = 240
FINE = SRC_LON // DEST_MERIDIANS
VARS = 8
BAND = 22
TILE = 4
OVER = 10
EDGE = 3
MID = BAND - 2 * EDGE
ROWS = BAND + 2 * EDGE
SPAN = BAND + EDGE
BINS = 16
HALF = BINS // 2
DAYS = 32
SLOTS = 4
FLAT = VARS * TILE
EDGE_LIMIT = 52
MID_LIMIT = 50
CODE_RATE = 10.0
CODE_BASE = 120.0
SUM_SCALE = 64.0
SUM_FLOOR = 2.0**-126


def shifted(value, step):
    slots = lax.axis_size("slot")
    return lax.ppermute(value, "slot", [(i, (i + step) % slots) for i in range(slots)])


def fill_table(table_ref):
    lines = 96
    line = lax.broadcasted_iota(jnp.int32, (lines, DEST_MERIDIANS), 0)
    start = FINE * lax.broadcasted_iota(jnp.int32, (lines, DEST_MERIDIANS), 1)
    for first in range(0, SRC_LON, lines):
        place = line + first - start
        inside = (place >= 0) & (place < FINE)
        table_ref[first : first + lines] = jnp.where(inside, 1.0, 0.0).astype(jnp.bfloat16)


def lon_mean(rows, table):
    flat = rows.reshape(-1, SRC_LON)
    total = jnp.dot(flat, table, preferred_element_type=jnp.float32)
    return (total * (1.0 / FINE)).astype(jnp.bfloat16).reshape(*rows.shape[:-1], DEST_MERIDIANS)


def params(mebibytes):
    return pltpu.CompilerParams(vmem_limit_bytes=mebibytes * 1024 * 1024)


def cost(microseconds):
    return pl.CostEstimate(
        flops=0, bytes_accessed=int(microseconds * 3 * 10**6), transcendentals=0
    )


def edge_kernel(field_ref, cross_ref, inner_ref, buf, table_buf, sems):
    odd = lax.rem(lax.axis_index("lat"), 2)
    firsts = (odd * (BAND - EDGE), (1 - odd) * (BAND - EDGE))
    outs = (cross_ref, inner_ref)
    jobs = []
    for n, first in enumerate(firsts):
        for part in range(2):
            some = pl.ds(part * HALF, HALF)
            copy = pltpu.make_async_copy(
                field_ref.at[some, pl.ds(first, EDGE)], buf.at[n, some], sems.at[2 * n + part]
            )
            copy.start()
            jobs.append((copy, n, slice(part * HALF, (part + 1) * HALF)))
    fill_table(table_buf)
    for copy, n, some in jobs:
        copy.wait()
        for s in range(some.start, some.stop, 4):
            outs[n][s : s + 4] = lon_mean(buf[n, s : s + 4], table_buf[...])


def edge_rows(field):
    vmem = pl.BlockSpec(memory_space=pltpu.VMEM)
    return pl.pallas_call(
        edge_kernel,
        in_specs=[pl.BlockSpec(memory_space=pl.ANY)],
        out_specs=[vmem] * 2,
        out_shape=[jax.ShapeDtypeStruct((BINS, EDGE, VARS, DEST_MERIDIANS), jnp.bfloat16)] * 2,
        scratch_shapes=[
            pltpu.VMEM((2, BINS, EDGE, VARS, SRC_LON), jnp.bfloat16),
            pltpu.VMEM((SRC_LON, DEST_MERIDIANS), jnp.bfloat16),
            pltpu.SemaphoreType.DMA((4,)),
        ],
        compiler_params=params(EDGE_LIMIT),
        cost_estimate=cost(2),
        name="edge_rows",
    )(field)


def mid_kernel(
    field_ref, index_ref, extent_ref, count_ref, out_ref, weights_ref,
    buf, table_buf, index_buf, extent_buf, count_buf, sems, small_sems,
):
    parts = sems.shape[0]
    size = BINS // parts
    block = 2
    lists = ((index_ref, index_buf), (extent_ref, extent_buf), (count_ref, count_buf))
    loads = [pltpu.make_async_copy(a, b, small_sems.at[n]) for n, (a, b) in enumerate(lists)]
    copies = []
    for n in range(parts):
        some = pl.ds(n * size, size)
        copies.append(
            pltpu.make_async_copy(field_ref.at[some, pl.ds(EDGE, MID)], buf.at[some], sems.at[n])
        )
    for copy in loads + copies:
        copy.start()
    fill_table(table_buf)
    for copy in loads:
        copy.wait()
    weights_ref[...] = weight_matrix(index_buf, extent_buf, count_buf)
    for first in range(0, BINS, block):
        if first % size == 0:
            copies[first // size].wait()
        some = slice(first, first + block)
        out_ref[some] = lon_mean(buf[some], table_buf[...])


def mid_rows(field, index, extent, count):
    parts = 4
    hbm = pl.BlockSpec(memory_space=pl.ANY)
    vmem = pl.BlockSpec(memory_space=pltpu.VMEM)
    return pl.pallas_call(
        mid_kernel,
        in_specs=[hbm] * 4,
        out_specs=[vmem] * 2,
        out_shape=[
            jax.ShapeDtypeStruct((BINS, MID, VARS, DEST_MERIDIANS), jnp.bfloat16),
            jax.ShapeDtypeStruct((3 * FLAT, ROWS * VARS), jnp.bfloat16),
        ],
        scratch_shapes=[
            pltpu.VMEM((BINS, MID, VARS, SRC_LON), jnp.bfloat16),
            pltpu.VMEM((SRC_LON, DEST_MERIDIANS), jnp.bfloat16),
            pltpu.SMEM((TILE, OVER), jnp.int32),
            pltpu.SMEM((TILE, OVER), jnp.float32),
            pltpu.SMEM((TILE,), jnp.int32),
            pltpu.SemaphoreType.DMA((parts,)),
            pltpu.SemaphoreType.DMA((3,)),
        ],
        compiler_params=params(MID_LIMIT),
        cost_estimate=cost(4),
        name="mid_rows",
    )(field, index, extent, count)


def encode(value):
    size = jnp.exp2(CODE_RATE * jnp.abs(value) - CODE_BASE)
    return jnp.where(value < 0, -size, size).astype(jnp.bfloat16)


def decode(code):
    wide = code.astype(jnp.float32)
    size = (jnp.log2(jnp.abs(wide)) + CODE_BASE) * (1.0 / CODE_RATE)
    size = jnp.where(jnp.abs(wide) > 2.0**-CODE_BASE, size, 0.0)
    return jnp.where(wide < 0, -size, size)


def weight_matrix(index_ref, extent_ref, count_ref):
    lat = lax.axis_index("lat")
    odd = lax.rem(lat, 2) == 1
    line = lax.broadcasted_iota(jnp.int32, (FLAT, ROWS * VARS), 0)
    lane = lax.broadcasted_iota(jnp.int32, (FLAT, ROWS * VARS), 1)
    place = jnp.where(line // TILE == lane % VARS, lane // VARS, -1)
    dense = jnp.zeros((FLAT, ROWS * VARS), jnp.float32)
    sums = jnp.ones((FLAT, ROWS * VARS), jnp.float32)
    for t in range(TILE):
        here = line % TILE == t
        spot = jnp.where(here, place, -1)
        total = jnp.float32(0.0)
        for k in range(OVER):
            value = jnp.where(k < count_ref[t], extent_ref[t, k], jnp.float32(0.0))
            total = total + value
            row = index_ref[t, k] - lat * BAND
            inside = (row >= EDGE) & (row < BAND - EDGE)
            shift = jnp.where(inside, 0, jnp.where(row < 0, SPAN, -SPAN))
            shift = jnp.where((row >= 0) & (row < EDGE), BAND - EDGE, shift)
            shift = jnp.where((row >= BAND - EDGE) & (row < BAND), EDGE - BAND, shift)
            column = row + EDGE + jnp.where(odd, shift, 0)
            dense = dense + jnp.where(spot == column, value, 0.0)
        sums = jnp.where(here, total, sums)
    dense = dense / sums
    high = dense.astype(jnp.bfloat16)
    rest = dense - high.astype(jnp.float32)
    middle_part = rest.astype(jnp.bfloat16)
    low = (rest - middle_part.astype(jnp.float32)).astype(jnp.bfloat16)
    return jnp.concatenate([high, middle_part, low], axis=0)


def climate_kernel(
    weights_ref, cross_ref, cross_own, mid_ref, inner_own, inner_ref, low_ref, high_ref
):
    weights = weights_ref[...]
    refs = (cross_ref, cross_own, mid_ref, inner_own, inner_ref)
    for s in range(BINS):
        rows = jnp.concatenate([ref[s] for ref in refs], axis=0)
        rows = rows.reshape(ROWS * VARS, DEST_MERIDIANS)
        parts = jnp.dot(weights, rows, preferred_element_type=jnp.float32)
        value = parts[:FLAT] + parts[FLAT : 2 * FLAT] + parts[2 * FLAT :]
        out_ref = low_ref if s < HALF else high_ref
        out_ref[s % HALF] = encode(value)


def climate_code(*arrays):
    vmem = pl.BlockSpec(memory_space=pltpu.VMEM)
    return pl.pallas_call(
        climate_kernel,
        in_specs=[vmem] * 6,
        out_specs=[vmem] * 2,
        out_shape=[jax.ShapeDtypeStruct((HALF, FLAT, DEST_MERIDIANS), jnp.bfloat16)] * 2,
        compiler_params=params(8),
        cost_estimate=cost(1),
        name="climate",
    )(*arrays)


def days_kernel(fore_ref, obs_ref, fore_out, obs_out, error_out):
    slot = lax.axis_index("slot")
    for k in range(SLOTS):
        lead = lax.rem(slot + k, SLOTS)

        def step(d, squared):
            fore = fore_ref[d, lead].astype(jnp.float32).reshape(FLAT, DEST_MERIDIANS)
            obs = obs_ref[d, lead].astype(jnp.float32).reshape(FLAT, DEST_MERIDIANS)
            fore_out[k, d] = fore
            obs_out[k, d] = obs
            error = fore - obs
            return squared + error * error

        zero = jnp.zeros((FLAT, DEST_MERIDIANS), jnp.float32)
        error_out[k] = lax.fori_loop(0, DAYS, step, zero, unroll=2)


def relaid_days(fore, obs):
    vmem = pl.BlockSpec(memory_space=pltpu.VMEM)
    grid = jax.ShapeDtypeStruct((SLOTS, DAYS, FLAT, DEST_MERIDIANS), jnp.float32)
    return pl.pallas_call(
        days_kernel,
        in_specs=[vmem] * 2,
        out_specs=[vmem] * 3,
        out_shape=[grid, grid, jax.ShapeDtypeStruct((SLOTS, FLAT, DEST_MERIDIANS), jnp.float32)],
        compiler_params=params(20),
        cost_estimate=cost(2),
        name="days",
    )(fore, obs)


def decode_kernel(*refs):
    near_ref = refs[-1]
    for n, code_ref in enumerate(refs[:-1]):
        near_ref[n * HALF : (n + 1) * HALF] = decode(code_ref[...])


def decoded(*codes):
    vmem = pl.BlockSpec(memory_space=pltpu.VMEM)
    return pl.pallas_call(
        decode_kernel,
        in_specs=[vmem] * len(codes),
        out_specs=vmem,
        out_shape=jax.ShapeDtypeStruct((len(codes) * HALF, FLAT, DEST_MERIDIANS), jnp.float32),
        compiler_params=params(8),
        cost_estimate=cost(1),
        name="decode",
    )(*codes)


def encode_sum(value):
    scaled = value * SUM_SCALE
    square = scaled * scaled
    power = square * square * square
    return jnp.where(value < 0, -power, power).astype(jnp.bfloat16)


def decode_sum(code):
    wide = code.astype(jnp.float32)
    size = jnp.maximum(jnp.abs(wide), SUM_FLOOR)
    root = jnp.exp2(jnp.log2(size) * (1.0 / 6.0)) * (1.0 / SUM_SCALE)
    root = jnp.where(wide == 0, 0.0, root)
    return jnp.where(wide < 0, -root, root)


def lead_sums(k, bins_ref, clim_ref, fore_ref, obs_ref, error_ref, out_ref, kept):
    slot = lax.axis_index("slot")
    lead = lax.rem(slot + k, SLOTS)
    first = slot * BINS
    half = FLAT // 2
    for h in range(2):
        some = slice(h * half, (h + 1) * half)

        def step(d, sums):
            cross, fore_sq, true_sq = sums
            clim = clim_ref[(bins_ref[lead, d] - first) & (SLOTS * BINS - 1), some]
            fore_anom = fore_ref[k, d, some] - clim
            true_anom = obs_ref[k, d, some] - clim
            return (
                cross + fore_anom * true_anom,
                fore_sq + fore_anom * fore_anom,
                true_sq + true_anom * true_anom,
            )

        zero = jnp.zeros((half, DEST_MERIDIANS), jnp.float32)
        sums = lax.fori_loop(0, DAYS, step, (zero,) * 3, unroll=16)
        for n, value in enumerate(sums):
            out_ref[n + 1, some] = kept(value)
    out_ref[0] = kept(error_ref[k])


def others_kernel(
    bins_ref, near_ref, low_ref, high_ref, fore_ref, obs_ref, error_ref,
    one_ref, two_ref, three_ref, clim_ref,
):
    clim_ref[: 2 * BINS] = near_ref[: 2 * BINS]
    clim_ref[3 * BINS :] = near_ref[2 * BINS :]
    clim_ref[2 * BINS : 2 * BINS + HALF] = decode(low_ref[...])
    clim_ref[2 * BINS + HALF : 3 * BINS] = decode(high_ref[...])
    for k, out_ref in ((1, one_ref), (2, two_ref), (3, three_ref)):
        lead_sums(k, bins_ref, clim_ref, fore_ref, obs_ref, error_ref, out_ref, encode_sum)


def mine_kernel(
    bins_ref, scale_ref, clim_ref, fore_ref, obs_ref, error_ref, out_ref, scale_out
):
    lat = lax.axis_index("lat")
    line = lax.broadcasted_iota(jnp.int32, (FLAT, DEST_MERIDIANS), 0)
    scale = jnp.zeros((FLAT, DEST_MERIDIANS), jnp.float32)
    for t in range(TILE):
        scale = jnp.where(line % TILE == t, scale_ref[lat * TILE + t], scale)
    scale_out[...] = scale
    lead_sums(0, bins_ref, clim_ref, fore_ref, obs_ref, error_ref, out_ref, lambda value: value)


def other_sums(bins, near, low, high, fore, obs, error):
    vmem = pl.BlockSpec(memory_space=pltpu.VMEM)
    code = jax.ShapeDtypeStruct((4, FLAT, DEST_MERIDIANS), jnp.bfloat16)
    whole = jax.ShapeDtypeStruct((SLOTS * BINS, FLAT, DEST_MERIDIANS), jnp.float32)
    return pl.pallas_call(
        others_kernel,
        in_specs=[pl.BlockSpec(memory_space=pltpu.SMEM)] + [vmem] * 6,
        out_specs=[vmem] * 4,
        out_shape=[code, code, code, whole],
        compiler_params=params(16),
        cost_estimate=cost(3),
        name="other_sums",
    )(bins, near, low, high, fore, obs, error)


def lat_weights():
    phi = (np.arange(DEST_PARALLELS, dtype=np.float32) + np.float32(0.5)) * np.float32(
        math.pi / DEST_PARALLELS
    ) - np.float32(0.5 * math.pi)
    cosine = np.cos(phi).astype(np.float32)
    return jnp.asarray(cosine / cosine.mean(dtype=np.float32))


def my_sums(bins, clim, fore, obs, error):
    smem = pl.BlockSpec(memory_space=pltpu.SMEM)
    vmem = pl.BlockSpec(memory_space=pltpu.VMEM)
    return pl.pallas_call(
        mine_kernel,
        in_specs=[smem] * 2 + [vmem] * 4,
        out_specs=[vmem] * 2,
        out_shape=[
            jax.ShapeDtypeStruct((4, FLAT, DEST_MERIDIANS), jnp.float32),
            jax.ShapeDtypeStruct((FLAT, DEST_MERIDIANS), jnp.float32),
        ],
        compiler_params=params(20),
        cost_estimate=cost(1),
        name="my_sums",
    )(bins, lat_weights(), clim, fore, obs, error)


def joined_kernel(one_ref, two_ref, own_ref, out_ref):
    out_ref[...] = own_ref[...] + decode_sum(one_ref[...]) + decode_sum(two_ref[...])


def joined(one, two, own):
    vmem = pl.BlockSpec(memory_space=pltpu.VMEM)
    return pl.pallas_call(
        joined_kernel,
        in_specs=[vmem] * 3,
        out_specs=vmem,
        out_shape=jax.ShapeDtypeStruct((4, FLAT, DEST_MERIDIANS), jnp.float32),
        compiler_params=params(8),
        cost_estimate=cost(1),
        name="joined",
    )(one, two, own)


def maps_kernel(three_ref, joined_ref, scale_ref, rmse_ref, acc_ref):
    total = joined_ref[...] + decode_sum(three_ref[...])
    rmse = jnp.sqrt(scale_ref[...] * total[0] / (DAYS * SLOTS))
    acc = total[1] / jnp.sqrt(total[2] * total[3] + 1e-06)
    rmse_ref[0] = rmse.reshape(VARS, TILE, DEST_MERIDIANS)
    acc_ref[0] = acc.reshape(VARS, TILE, DEST_MERIDIANS)


def maps(*arrays):
    vmem = pl.BlockSpec(memory_space=pltpu.VMEM)
    shape = jax.ShapeDtypeStruct((1, VARS, TILE, DEST_MERIDIANS), jnp.float32)
    return pl.pallas_call(
        maps_kernel,
        in_specs=[vmem] * 3,
        out_specs=[vmem] * 2,
        out_shape=[shape] * 2,
        compiler_params=params(8),
        cost_estimate=cost(1),
        name="maps",
    )(*arrays)


def body(normals, index, extent, count, bins, prognosis, analysis):
    field = jnp.transpose(normals, (0, 2, 1, 3))
    cross_own, inner_own = edge_rows(field)
    devices, slots = lax.axis_size("lat"), lax.axis_size("slot")
    meets = [(i * slots + x, (i + 1) * slots + x) for i in range(1, devices - 1, 2) for x in range(slots)]
    meets += [(i * slots + x, i * slots + x + 1) for i in (0, devices - 1) for x in range(0, slots, 2)]
    meets = [pair for i, j in meets for pair in ((i, j), (j, i))]
    cross = lax.ppermute(cross_own, ("lat", "slot"), meets)
    inner = lax.ppermute(inner_own, "lat", [(i, i ^ 1) for i in range(devices)])
    mid, weights = mid_rows(field, index, extent, count)
    low, high = climate_code(weights, cross, cross_own, mid, inner_own, inner)
    left_low = shifted(low, 1)
    right_high = shifted(high, -1)
    left_high = shifted(high, 1)
    right_low = shifted(low, -1)
    far_low = shifted(left_low, 1)
    far_high = shifted(right_high, -1)
    fore, obs, error = relaid_days(prognosis, analysis)
    near = decoded(low, high, right_low, right_high, left_low, left_high)
    wanted = jnp.transpose(bins)
    to_one, to_two, to_three, clim = other_sums(
        wanted, near, far_low, far_high, fore, obs, error
    )
    two = shifted(to_two, 2)
    one = shifted(to_one, 1)
    three = shifted(to_three, 3)
    mine, scale = my_sums(wanted, clim, fore, obs, error)
    return tuple(maps(three, joined(one, two, mine), scale))


def solution(mesh):
    placed = (
        P("slot", None, "lat", None),
        P("lat", None),
        P("lat", None),
        P("lat"),
        P("slot", None),
        P("slot", None, None, "lat", None),
        P("slot", None, None, "lat", None),
    )

    return jax.shard_map(
        body,
        mesh=mesh,
        in_specs=placed,
        out_specs=(P("slot", None, "lat", None), P("slot", None, "lat", None)),
        check_vma=False,
    )
```
